32 devices in a mesh: gx: 8 (over y, x, core), gy: 4 (over z).
Axes of the slice: x: 2, y: 2, z: 4, core: 2. Of those that a mesh axis runs over, the one named last changes fastest.
Arguments:
- features: bfloat16 [8, 4, 512, 128], P('gx', 'gy'), may hold values from -6 to 6
- cotangent: bfloat16 [8, 4, 512, 128], P('gx', 'gy'), may hold values from -6 to 6
- weight_one: bfloat16 [27, 128, 128], replicated, may hold values from -0.125 to 0.125
- weight_two: bfloat16 [27, 128, 128], replicated, may hold values from -0.125 to 0.125
- block_count: int32 [8, 4], P('gx', 'gy'), may hold values from 4 to 8, as said below
- send_list: int32 [8, 4, 8, 4], P('gx', 'gy'), may hold values from 0 to 7, as said below
- rulebook: int32 [8, 4, 27, 512], P('gx', 'gy'), may hold values from 0 to 2560, as said below
Outputs:
- output: bfloat16 [8, 4, 512, 128], P('gx', 'gy')
- grad_features: bfloat16 [8, 4, 512, 128], P('gx', 'gy')
- grad_one: float32 [27, 128, 128], P(None, 'gx')
- grad_two: float32 [27, 128, 128], P(None, 'gx')
The draws below stay inside these ranges and needn't reach their ends.
Inputs may be any that keep to these rules, and one draw needn't show every extreme that they name: The active blocks of a device are its first block_count blocks; some device has 8. send_list[a, b, e] lists the 4 blocks that device (a, b) sends toward the device at direction d_e; every entry is an active block of the sender; entries may repeat. rulebook[a, b, k, i] is a row of device (a, b)'s extended table; 2560 is the zero row and means no neighbour at that offset. Rows of inactive blocks hold 2560 at every offset; for an active row, offset 13 is the row itself; every other entry below 2560 is an active row of the device or a row of the slot of a neighbouring device that exists.
All inputs are finite; a program needn't handle non-finite values.
Results may differ from the reference program's by a relative error of at most 0.0055.
Values may be sent and summed in bfloat16 or wider, within the bound.
A program may use at most 128 MiB of HBM per device.

```python
import jax
import jax.numpy as jnp
import numpy as np
from jax import lax

C = 128
BLK = 64
NBLK = 8
SEND = 4
EXT = 2560
DEVS = 32
N_GX = 8
N_GY = 4


STEPS_X = np.array([-1, -1, -1, 0, 0, 1, 1, 1], dtype=np.int32)


STEPS_Y = np.array([-1, 0, 1, -1, 1, -1, 0, 1], dtype=np.int32)


def block_layout(key):
    device_total = N_GX * N_GY
    counts = jax.random.randint(jax.random.fold_in(key, 11), (device_total,), NBLK // 2, NBLK + 1)
    fullest = jax.random.randint(jax.random.fold_in(key, 12), (), 0, device_total)
    counts = counts.at[fullest].set(NBLK)
    return (counts.reshape(N_GX, N_GY).astype(jnp.int32), fullest)


def draw_block_count(key, part):
    counts, fullest = block_layout(key)
    return counts


def draw_send_list(key, part):
    counts, fullest = block_layout(key)
    raw_bits = jax.random.randint(jax.random.fold_in(key, 13), (N_GX, N_GY, 8, SEND), 0, 1 << 20)
    listed = raw_bits % counts[:, :, None, None]
    flat_list = listed.reshape(N_GX * N_GY, 8, SEND)
    flat_list = flat_list.at[fullest, 0, 0].set(NBLK - 1)
    flat_list = flat_list.at[fullest, 1, 0].set(0)
    return flat_list.reshape(N_GX, N_GY, 8, SEND).astype(jnp.int32)


def draw_rulebook(key, part):
    counts, fullest = block_layout(key)
    row_total = NBLK * BLK
    table_end = row_total + 8 * SEND * BLK
    shape_all = (N_GX, N_GY, 27, row_total)
    raw_bits = jax.random.randint(jax.random.fold_in(key, 14), shape_all, 0, 1 << 24)
    direction = jax.random.randint(jax.random.fold_in(key, 15), shape_all, 0, 8)
    slot_row = jax.random.randint(jax.random.fold_in(key, 16), shape_all, 0, SEND * BLK)
    place_x = jax.lax.broadcasted_iota(jnp.int32, shape_all, 0)
    place_y = jax.lax.broadcasted_iota(jnp.int32, shape_all, 1)
    offsets = jax.lax.broadcasted_iota(jnp.int32, shape_all, 2)
    row_ids = jax.lax.broadcasted_iota(jnp.int32, shape_all, 3)
    kinds = raw_bits % 8
    picked = raw_bits // 8
    live_rows = counts[:, :, None, None] * BLK
    local_row = picked % live_rows
    other_x = place_x + jnp.asarray(STEPS_X)[direction]
    other_y = place_y + jnp.asarray(STEPS_Y)[direction]
    exists = (other_x >= 0) & (other_x < N_GX) & (other_y >= 0) & (other_y < N_GY)
    halo_row = row_total + direction * (SEND * BLK) + slot_row
    chosen = jnp.where(kinds < 4, table_end, jnp.where((kinds >= 6) & exists, halo_row, local_row))
    chosen = jnp.where(offsets == 13, row_ids, chosen)
    active = row_ids // BLK < counts[:, :, None, None]
    return jnp.where(active, chosen, table_end).astype(jnp.int32)


def strengthened(values, key, source, target, blocks, factor):
    def block_of(dim):
        return (jnp.arange(values.shape[dim]) // (values.shape[dim] // blocks)).reshape((-1,) + (1,) * (values.ndim - 1 - dim))

    near = jax.random.permutation(key, blocks)[block_of(target)]
    other_side = (block_of(target) + blocks // 2) % blocks
    return jnp.where((block_of(source) == near) | (block_of(source) == other_side), factor * values, values)


def block_scale(own_key, extent, pieces, low, top_value):
    level = 1.0
    for axis_at, blocks in pieces:
        draws = jax.random.uniform(jax.random.fold_in(jax.random.fold_in(own_key, 6), axis_at), (blocks,), jnp.float32, low / len(pieces), top_value / len(pieces))
        level = level * jnp.repeat(jnp.exp(draws), extent[axis_at] // blocks).reshape((-1,) + (1,) * (len(extent) - 1 - axis_at))
    return level


def gaussian(rng, dims, spread, reach, split=(), kind=jnp.bfloat16):
    entries = spread * jax.random.normal(rng, dims, jnp.float32)
    if split:
        entries = entries * block_scale(rng, dims, split, -0.22, 0.18)
    return jnp.clip(entries, -reach, reach).astype(kind)


def noise_with(rng, extent, width, most, shards, heavy, kind=jnp.bfloat16):
    values = width * jax.random.normal(rng, extent, jnp.float32)
    if shards:
        values = values * block_scale(rng, extent, shards, -0.22, 0.18)
    return jnp.clip(strengthened(values, jax.random.fold_in(rng, 3), *heavy), -most, most).astype(kind)


def setup_inputs(seed: int = 0) -> dict:
    key_of = jax.random.split(jax.random.key(seed), 8)
    features = noise_with(key_of[0], (N_GX, N_GY, NBLK * BLK, C), 1.0, 6.0, ((0, 8), (1, 4)), (0, 3, 8, 2.0))
    cotangent = gaussian(key_of[1], (N_GX, N_GY, NBLK * BLK, C), 1.0, 6.0, ((0, 8), (1, 4)))
    weight_one = gaussian(key_of[2], (27, C, C), (14 * C) ** -0.5, 0.125)
    weight_two = gaussian(key_of[3], (27, C, C), (14 * C) ** -0.5, 0.125)
    block_count = draw_block_count(jax.random.fold_in(key_of[7], 71), 0)
    send_list = draw_send_list(jax.random.fold_in(key_of[7], 71), 0)
    rulebook = draw_rulebook(jax.random.fold_in(key_of[7], 71), 0)
    return dict(features=features, cotangent=cotangent, weight_one=weight_one, weight_two=weight_two, block_count=block_count, send_list=send_list, rulebook=rulebook)


DIRECTIONS = ((-1, -1), (-1, 0), (-1, 1), (0, -1), (0, 1), (1, -1), (1, 0), (1, 1))

def neighbour(source, step_x, step_y):
    padding = [(1, 1), (1, 1)] + [(0, 0)] * (source.ndim - 2)
    padded = jnp.pad(source, padding)
    return padded[1 + step_x:1 + step_x + N_GX, 1 + step_y:1 + step_y + N_GY]

def take_rows(lookup, chosen):
    return jax.vmap(jax.vmap(lambda table_rows, picked: table_rows[picked]))(lookup, chosen)

def extend_field(field, send_list):
    block_rows = field.reshape(N_GX, N_GY, NBLK, BLK, C)
    outgoing = jax.vmap(jax.vmap(lambda blocks, listed: blocks[listed]))(block_rows, send_list)
    halos = [neighbour(outgoing[:, :, 7 - index_j], step_x, step_y) for index_j, (step_x, step_y) in enumerate(DIRECTIONS)]
    halo_rows = jnp.stack(halos, 2).reshape(N_GX, N_GY, 8 * SEND * BLK, C)
    zero_row = jnp.zeros((N_GX, N_GY, 1, C), field.dtype)
    return jnp.concatenate((field, halo_rows, zero_row), 2)

def conv_forward(extended, rulebook, weight):
    rule_sets = jnp.moveaxis(rulebook, 2, 0)

    def add_offset(totals, item):
        indices, matrix = item
        gathered = take_rows(extended, indices)
        return (totals + jnp.dot(gathered, matrix, preferred_element_type=jnp.float32), None)
    start = jnp.zeros((N_GX, N_GY, NBLK * BLK, C), jnp.float32)
    totals, ignored = lax.scan(add_offset, start, (rule_sets, weight))
    return totals

def conv_transpose(grads, rulebook, weight, send_list):
    rule_sets = jnp.moveaxis(rulebook, 2, 0)

    def add_offset(totals, item):
        indices, matrix = item
        terms = jnp.dot(grads, matrix.T, preferred_element_type=jnp.float32)
        totals = jax.vmap(jax.vmap(lambda table_rows, picked, values: table_rows.at[picked].add(values)))(totals, indices, terms)
        return (totals, None)
    start = jnp.zeros((N_GX, N_GY, EXT + 1, C), jnp.float32)
    totals, ignored = lax.scan(add_offset, start, (rule_sets, weight))
    row_total = NBLK * BLK
    local_blocks = totals[:, :, :row_total].reshape(N_GX, N_GY, NBLK, BLK, C)
    halo_part = totals[:, :, row_total:EXT].astype(jnp.bfloat16)
    halo_part = lax.optimization_barrier(halo_part).astype(jnp.float32)
    halo_part = halo_part.reshape(N_GX, N_GY, 8, SEND, BLK, C)
    for index_j, (step_x, step_y) in enumerate(DIRECTIONS):
        incoming = neighbour(halo_part[:, :, index_j], -step_x, -step_y)
        targets = send_list[:, :, 7 - index_j]
        local_blocks = jax.vmap(jax.vmap(lambda blocks, listed, values: blocks.at[listed].add(values)))(local_blocks, targets, incoming)
    return local_blocks.reshape(N_GX, N_GY, row_total, C)

def weight_grad(extended, rulebook, grads):
    rule_sets = jnp.moveaxis(rulebook, 2, 0)
    flat_grads = grads.reshape(-1, C)

    def one_offset(carried, indices):
        gathered = take_rows(extended, indices).reshape(-1, C)
        return (carried, jnp.dot(gathered.T, flat_grads, preferred_element_type=jnp.float32))
    ignored, stacked = lax.scan(one_offset, jnp.zeros((), jnp.float32), rule_sets)
    return stacked

def reference(features, cotangent, weight_one, weight_two, block_count, send_list, rulebook):
    positions = jnp.arange(NBLK * BLK).astype(jnp.int32) // BLK
    live = (positions[None, None, :] < block_count[:, :, None])[..., None]
    live_float = live.astype(jnp.float32)
    live_half = live.astype(jnp.bfloat16)
    masked = features * live_half
    ext_input = extend_field(masked, send_list)
    first_pre = conv_forward(ext_input, rulebook, weight_one) * live_float
    hidden = jax.nn.silu(first_pre).astype(jnp.bfloat16)
    ext_hidden = extend_field(hidden, send_list)
    output = (conv_forward(ext_hidden, rulebook, weight_two) * live_float).astype(jnp.bfloat16)
    upstream = cotangent * live_half
    grad_hidden = conv_transpose(upstream, rulebook, weight_two, send_list)
    sigmoid_pre = jax.nn.sigmoid(first_pre)
    grad_pre = (grad_hidden * sigmoid_pre * (1.0 + first_pre * (1.0 - sigmoid_pre)) * live_float).astype(jnp.bfloat16)
    grad_features = (conv_transpose(grad_pre, rulebook, weight_one, send_list) * live_float).astype(jnp.bfloat16)
    grad_two = weight_grad(ext_hidden, rulebook, upstream) / DEVS
    grad_one = weight_grad(ext_input, rulebook, grad_pre) / DEVS
    return (output, grad_features, grad_one, grad_two)
```

```python
import functools

import jax
import jax.numpy as jnp
from jax import lax
from jax.experimental import pallas as pl
from jax.experimental.pallas import tpu as pltpu
from jax.sharding import PartitionSpec as P

BLK = 64
EARLY = 6
F32 = jnp.float32
BF16 = jnp.bfloat16
I16 = jnp.int16
MESH = pl.DeviceIdType.MESH
DIRECTIONS = ((-1, -1), (-1, 0), (-1, 1), (0, -1), (0, 1), (1, -1), (1, 0), (1, 1))

VM = pl.BlockSpec(memory_space=pltpu.VMEM)
SM = pl.BlockSpec(memory_space=pltpu.SMEM)
ANY = pl.BlockSpec(memory_space=pl.ANY)


def whole_kernel(
    nx, ny, groups,
    count, send, features, cotangent, rule, w1_in, w2_in,
    output, grad_input, grad_one, grad_two,
    feat, cot, rule3, w1, w2, flat, low, packed, index, masks,
    wide1, wide2, tall, field, hidden, upstream, grad, pre, gathered, buf, acc, own, sums,
    outs, backs, rets, gsend, prec, red, xrecv, ysend, yrecv,
    load_s, halo_ss, halo_rs, pss, prs, xss, xrs, yss, yrs,
):
    a, b = lax.axis_index("gx"), lax.axis_index("gy")
    nblk, blk, channels = field.shape
    rows = nblk * blk
    kernel = w1.shape[0]
    mid = kernel // 2
    per = send.shape[0]
    slot = per * blk
    chunk = channels // nx
    depth = acc.shape[0]
    first_slots = (depth - rows) // slot
    zero_row = rows + 8 * slot
    core = lax.rem(a, 2)
    chip = a // 2
    chips = nx // 2

    def exists(e):
        dx, dy = DIRECTIONS[e]
        x, y = a + dx, b + dy
        return (x >= 0) & (x < nx) & (y >= 0) & (y < ny)

    def place(e):
        dx, dy = DIRECTIONS[e]
        return (a + dx, b + dy)

    loads = [
        pltpu.make_async_copy(src, dst, load_s.at[n])
        for n, (src, dst) in enumerate((
            (features, feat), (rule, rule3), (cotangent, cot), (w2_in, w2), (w1_in, w1),
        ))
    ]
    for copy in loads:
        copy.start()

    barrier = pltpu.get_barrier_semaphore()
    for off in range(1, nx):
        pl.semaphore_signal(barrier, inc=1, device_id=(lax.rem(a + off, nx), b), device_id_type=MESH)
    for off in range(1, ny):
        pl.semaphore_signal(barrier, inc=1, device_id=(a, lax.rem(b + off, ny)), device_id_type=MESH)
    corners = (0, 2, 5, 7)
    for e in corners:
        dx, dy = DIRECTIONS[e]
        corner = (lax.rem(a + dx + nx, nx), lax.rem(b + dy + ny, ny))
        pl.semaphore_signal(barrier, inc=1, device_id=corner, device_id_type=MESH)

    def wide_view(wide, j):
        if j < first_slots:
            return wide.at[pl.ds(rows + j * slot, slot), pl.ds(0, channels)]
        return wide.at[pl.ds((j - first_slots) * slot, slot), pl.ds(channels, channels)]

    for j in range(8):
        @pl.when(jnp.logical_not(exists(j)))
        def _():
            blank = jnp.zeros((slot, channels), BF16)
            wide_view(wide1, j)[...] = blank
            wide_view(wide2, j)[...] = blank
            rets[0, j] = blank
            rets[1, j] = blank

    loads[0].wait()
    ids = lax.broadcasted_iota(jnp.int32, (rows, 1), 0)
    live = (ids < count[0, 0] * blk).astype(F32)
    masked32 = feat[...].astype(F32) * live
    masked = masked32.astype(BF16)
    field[...] = masked.reshape(nblk, blk, channels)
    wide1[:rows, :channels] = masked

    def ext_copy(x, e, wide):
        return pltpu.make_async_remote_copy(
            src_ref=outs.at[x, e], dst_ref=wide_view(wide, 7 - e),
            send_sem=halo_ss.at[x, e], recv_sem=halo_rs.at[x, 7 - e],
            device_id=place(e), device_id_type=MESH,
        )

    def back_copy(x, j):
        return pltpu.make_async_remote_copy(
            src_ref=backs.at[x, j], dst_ref=rets.at[x, j],
            send_sem=halo_ss.at[2 + x, j], recv_sem=halo_rs.at[2 + x, j],
            device_id=place(j), device_id_type=MESH,
        )

    def pack_ext(x, source):
        for e in range(8):
            for s in range(per):
                outs[x, e, s * blk : (s + 1) * blk, :] = source[send[s, e]]

    def start_ext(x, wide):
        for e in range(8):
            @pl.when(exists(e))
            def _():
                ext_copy(x, e, wide).start()

    def wait_ext(x, wide):
        for e in range(8):
            @pl.when(exists(7 - e))
            def _():
                ext_copy(x, e, wide).wait_recv()

    def fill_tall(wide):
        tall[:rows] = wide[:rows, :channels].astype(F32)
        for j in range(8):
            tall[rows + j * slot : rows + (j + 1) * slot] = wide_view(wide, j)[...].astype(F32)

    def send_back(x):
        for j in range(8):
            backs[x, j] = wide_view(acc, j)[...].astype(BF16)

            @pl.when(exists(j))
            def _():
                back_copy(x, j).start()

    def wait_back(x):
        for j in range(8):
            @pl.when(exists(7 - j))
            def _():
                back_copy(x, j).wait_recv()

    def returned_total(x):
        part = 32
        for h in range(0, blk, part):
            totals = [own[n * blk + h : n * blk + h + part, :] for n in range(nblk)]
            for e in range(8):
                for s in range(per):
                    value = rets[x, e, s * blk + h : s * blk + h + part, :].astype(F32)
                    target = send[s, 7 - e]
                    for n in range(nblk):
                        totals[n] += jnp.where(target == n, 1.0, 0.0) * value
            for n in range(nblk):
                own[n * blk + h : n * blk + h + part, :] = totals[n]

    pack_ext(0, field)
    pl.semaphore_wait(barrier, nx - 1 + ny - 1 + len(corners))
    start_ext(0, wide1)

    loads[1].wait()
    for k in range(kernel):
        flat[k : k + 1, :] = rule3[k]
    flat[kernel:, :] = jnp.full((flat.shape[0] - kernel, rows), zero_row, jnp.int32)
    book = flat[...]
    packed[...] = book[:, : rows // 2] + book[:, rows // 2 :] * 65536
    to_smem = pltpu.make_async_copy(packed, index, load_s.at[5])
    to_smem.start()
    second = book >= depth
    low[...] = jnp.where(second, book - depth, book)
    chosen = jnp.where(second, 1.0, 0.0).astype(BF16)
    shown = (flat.shape[0], 2 * channels)
    for s in range(mid):
        picks = jnp.where(
            lax.broadcasted_iota(jnp.int32, shown, 0)
            == jnp.where(lax.broadcasted_iota(jnp.int32, shown, 1) < channels, s, s + mid + 1),
            1.0, 0.0,
        ).astype(BF16)
        masks[s] = lax.dot_general(
            chosen, picks, (((0,), (0,)), ((), ())), preferred_element_type=F32
        ).astype(BF16)
    loads[2].wait()
    upstream[...] = (cot[...].astype(F32) * live).astype(BF16)
    tall[zero_row : zero_row + 8] = jnp.zeros((8, channels), F32)
    loads[3].wait()
    loads[4].wait()

    def pair(s):
        return (s, s + mid + 1)

    def stacked(w, s):
        return jnp.concatenate([w[k] for k in pair(s)], axis=0)

    def scatter(s, g, w):
        terms = lax.dot_general(
            g, stacked(w, s), (((1,), (1,)), ((), ())), preferred_element_type=F32
        ).astype(BF16)
        upper = terms * masks[s]
        lower = terms - upper
        values = jnp.concatenate(
            [
                jnp.concatenate(
                    [part[:, u * channels : (u + 1) * channels] for part in (lower, upper)], axis=1
                )
                for u in range(2)
            ],
            axis=0,
        )
        place_of = lax.broadcasted_iota(I16, (depth, rows), 0)
        hots = []
        for k in pair(s):
            wanted = jnp.broadcast_to(low[pl.ds(k, 1), :].astype(I16), (depth, rows))
            hots.append(jnp.where(place_of == wanted, jnp.ones((), BF16), jnp.zeros((), BF16)))
        acc[...] += jnp.dot(jnp.concatenate(hots, axis=1), values, preferred_element_type=F32)

    def scatter_first(g, w):
        acc[...] = jnp.zeros_like(acc)
        acc[:rows, :channels] = lax.dot_general(
            g, w[mid], (((1,), (1,)), ((), ())), preferred_element_type=F32
        )

    def gather(s):
        for u, k in enumerate(pair(s)):
            for n in range(rows // 2):
                word = index[k, n]
                buf[u, n : n + 1, :] = tall[pl.ds(jnp.bitwise_and(word, 65535), 1), :]
                other = n + rows // 2
                buf[u, other : other + 1, :] = tall[pl.ds(lax.shift_right_logical(word, 16), 1), :]
            gathered[k] = buf[u].astype(BF16)

    def both(s):
        return jnp.concatenate([gathered[k] for k in pair(s)], axis=1)

    def keep_partial(g, s, picks, rows_out):
        part = lax.dot_general(
            picks, rows_out, (((0,), (0,)), ((), ())), preferred_element_type=F32
        ).astype(BF16)
        for u in range(2):
            for p in range(nx):
                first = u * channels + p * chunk
                gsend[g, p % 2, p // 2, 1 + 2 * s + u] = part[first : first + chunk, :]

    def keep_first(g, rows_in, rows_out):
        part = lax.dot_general(
            rows_in, rows_out, (((0,), (0,)), ((), ())), preferred_element_type=F32
        ).astype(BF16)
        for p in range(nx):
            gsend[g, p % 2, p // 2, 0] = part[p * chunk : (p + 1) * chunk, :]

    def span(t):
        g, first, last = groups[t]
        return g, pl.ds(first, last - first)

    def pair_copy(t):
        g, qs = span(t)
        return pltpu.make_async_remote_copy(
            src_ref=gsend.at[g, 1 - core, :, qs], dst_ref=prec.at[g, :, qs],
            send_sem=pss.at[t], recv_sem=prs.at[t],
            device_id=(a + 1 - 2 * core, b), device_id_type=MESH,
        )

    def chip_copy(t, off):
        g, qs = span(t)
        peer = lax.rem(chip + off, chips)
        return pltpu.make_async_remote_copy(
            src_ref=red.at[g, peer, qs], dst_ref=xrecv.at[g, off, qs],
            send_sem=xss.at[t, off], recv_sem=xrs.at[t, off],
            device_id=(2 * peer + core, b), device_id_type=MESH,
        )

    def gy_copy(t, off):
        g, qs = span(t)
        return pltpu.make_async_remote_copy(
            src_ref=ysend.at[g, qs], dst_ref=yrecv.at[g, off, qs],
            send_sem=yss.at[t, off], recv_sem=yrs.at[t, off],
            device_id=(a, lax.rem(b + off, ny)), device_id_type=MESH,
        )

    def reduce_pair(t):
        g, qs = span(t)
        pair_copy(t).wait_recv()
        for n in range(chips):
            red[g, n, qs] = (gsend[g, core, n, qs].astype(F32) + prec[g, n, qs].astype(F32)).astype(BF16)
        for off in range(1, chips):
            chip_copy(t, off).start()

    def reduce_chips(t):
        g, qs = span(t)
        total = red[g, chip, qs].astype(F32)
        for off in range(1, chips):
            chip_copy(t, off).wait_recv()
            total += xrecv[g, off, qs].astype(F32)
        ysend[g, qs] = total.astype(BF16)
        for off in range(1, ny):
            gy_copy(t, off).start()

    def reduce_gy(t):
        g, first, last = groups[t]
        _, qs = span(t)
        for off in range(1, ny):
            gy_copy(t, off).wait_recv()
        mine = ysend[g, qs].astype(F32)
        others = [yrecv[g, off, qs].astype(F32) for off in range(1, ny)]
        total = jnp.zeros(mine.shape, F32)
        for source in range(ny):
            term = jnp.where(source == b, mine, 0.0)
            for off in range(1, ny):
                here = lax.rem(b - off + ny, ny) == source
                term = jnp.where(here, others[off - 1], term)
            total += term
        total = total * (1.0 / (nx * ny))
        out = (grad_one, grad_two)[g]
        for q in range(first, last):
            k = mid if q == 0 else (q - 1) // 2 + ((q - 1) % 2) * (mid + 1)
            out[k] = total[q - first]

    scatter_first(upstream[...], w2)

    @pl.loop(0, EARLY)
    def _(s):
        scatter(s, upstream[...], w2)

    wait_ext(0, wide1)
    fill_tall(wide1)
    to_smem.wait()
    pre[...] = jnp.dot(wide1[:rows, :channels], w1[mid], preferred_element_type=F32)

    def first_conv(s):
        pre[...] += jnp.dot(both(s), stacked(w1, s), preferred_element_type=F32)

    gather(0)

    @pl.loop(EARLY, mid)
    def _(s):
        first_conv(s - EARLY)
        scatter(s, upstream[...], w2)
        gather(s - EARLY + 1)

    send_back(0)
    own[...] = acc[:rows, :channels]

    @pl.loop(mid - EARLY + 1, mid)
    def _(s):
        first_conv(s - 1)
        gather(s)

    first_conv(mid - 1)
    v = pre[...] * live
    pre[...] = v
    hid = (v / (1.0 + jnp.exp(-v))).astype(BF16)
    hidden[...] = hid.reshape(nblk, blk, channels)
    wide2[:rows, :channels] = hid
    pack_ext(1, hidden)
    start_ext(1, wide2)

    wait_back(0)
    returned_total(0)
    v = pre[...]
    s = 1.0 / (1.0 + jnp.exp(-v))
    grad[...] = (own[...] * s * (1.0 + v * (1.0 - s)) * live).astype(BF16)

    keep_first(0, wide1[:rows, :channels], grad[...])

    @pl.loop(0, mid)
    def _(s):
        keep_partial(0, s, both(s), grad[...])

    pair_copy(0).start()
    scatter_first(grad[...], w1)

    @pl.loop(0, EARLY)
    def _(s):
        scatter(s, grad[...], w1)

    reduce_pair(0)
    wait_ext(1, wide2)
    fill_tall(wide2)
    sums[...] = jnp.dot(wide2[:rows, :channels], w2[mid], preferred_element_type=F32)
    keep_first(1, wide2[:rows, :channels], upstream[...])

    def second_conv(s):
        picks = both(s)
        sums[...] += jnp.dot(picks, stacked(w2, s), preferred_element_type=F32)
        keep_partial(1, s, picks, upstream[...])

    gather(0)

    @pl.loop(EARLY, mid)
    def _(s):
        second_conv(s - EARLY)
        scatter(s, grad[...], w1)
        gather(s - EARLY + 1)

    send_back(1)
    own[...] = acc[:rows, :channels]
    pair_copy(1).start()
    reduce_chips(0)

    half = mid - EARLY + 1 + (EARLY - 1) // 2

    @pl.loop(mid - EARLY + 1, half)
    def _(s):
        second_conv(s - 1)
        gather(s)

    reduce_pair(1)
    pair_copy(2).start()

    @pl.loop(half, mid)
    def _(s):
        second_conv(s - 1)
        gather(s)

    second_conv(mid - 1)
    pair_copy(3).start()
    reduce_pair(2)
    reduce_chips(1)
    output[...] = (sums[...] * live).astype(BF16)
    reduce_gy(0)
    reduce_pair(3)
    reduce_chips(2)
    wait_back(1)
    returned_total(1)
    grad_input[...] = (own[...] * live).astype(BF16)
    reduce_chips(3)
    for t in range(1, len(groups)):
        reduce_gy(t)

    for e in range(8):
        @pl.when(exists(e))
        def _():
            ext_copy(0, e, wide1).wait_send()
            ext_copy(1, e, wide2).wait_send()
            back_copy(0, e).wait_send()
            back_copy(1, e).wait_send()
    for t in range(len(groups)):
        pair_copy(t).wait_send()
        for off in range(1, chips):
            chip_copy(t, off).wait_send()
        for off in range(1, ny):
            gy_copy(t, off).wait_send()


def on_device(features, cotangent, weight_one, weight_two, block_count, send_list, rulebook):
    field, cot = features[0, 0], cotangent[0, 0]
    rows, channels = field.shape
    kernel = rulebook.shape[2]
    mid = kernel // 2
    send = send_list[0, 0].T
    rule = rulebook.reshape(kernel, 1, rows)
    slot = send.shape[0] * BLK
    nx, ny = lax.axis_size("gx"), lax.axis_size("gy")
    chunk = channels // nx
    depth = (rows + 8 * slot) // 2
    tall_rows = rows + 8 * slot + 8
    first = 1 + 2 * (mid - EARLY)
    second = first + 2 * ((EARLY - 1) // 2)
    groups = ((0, 0, kernel), (1, 0, first), (1, first, second), (1, second, kernel))
    shape = jax.ShapeDtypeStruct
    grads = shape((kernel, chunk, channels), F32)
    plain_f = pltpu.VMEM((rows, channels), F32)
    plain_b = pltpu.VMEM((rows, channels), BF16)
    blocks = pltpu.VMEM((rows // BLK, BLK, channels), BF16)
    halos = pltpu.VMEM((2, 8, slot, channels), BF16)
    wide = pltpu.VMEM((depth, 2 * channels), BF16)
    weights = pltpu.VMEM((kernel, channels, channels), BF16)
    high = -(-kernel // 8) * 8
    parts = len(groups)
    tile = (chunk, channels)
    sem = pltpu.SemaphoreType.DMA
    output, grad_input, one, two = pl.pallas_call(
        functools.partial(whole_kernel, nx, ny, groups),
        out_shape=(shape((rows, channels), BF16),) * 2 + (grads, grads),
        in_specs=[SM, SM] + [ANY] * 5,
        out_specs=(VM,) * 4,
        scratch_shapes=[
            plain_b, plain_b, pltpu.VMEM((kernel, 1, rows), jnp.int32), weights, weights,
            pltpu.VMEM((high, rows), jnp.int32), pltpu.VMEM((high, rows), jnp.int32),
            pltpu.VMEM((high, rows // 2), jnp.int32), pltpu.SMEM((high, rows // 2), jnp.int32),
            pltpu.VMEM((mid, rows, 2 * channels), BF16),
            wide, wide, pltpu.VMEM((tall_rows, channels), F32), blocks, blocks,
            plain_b, plain_b, plain_f, pltpu.VMEM((kernel, rows, channels), BF16),
            pltpu.VMEM((2, rows, channels), F32), pltpu.VMEM((depth, 2 * channels), F32),
            plain_f, plain_f, halos, halos, halos,
            pltpu.VMEM((2, 2, nx // 2, kernel) + tile, BF16),
            pltpu.VMEM((2, nx // 2, kernel) + tile, BF16),
            pltpu.VMEM((2, nx // 2, kernel) + tile, BF16),
            pltpu.VMEM((2, nx // 2, kernel) + tile, BF16),
            pltpu.VMEM((2, kernel) + tile, BF16),
            pltpu.VMEM((2, ny, kernel) + tile, BF16),
            sem((6,)), sem((4, 8)), sem((4, 8)), sem((parts,)), sem((parts,)),
            sem((parts, nx // 2)), sem((parts, nx // 2)), sem((parts, ny)), sem((parts, ny)),
        ],
        compiler_params=pltpu.CompilerParams(
            vmem_limit_bytes=56 << 20, collective_id=0, has_side_effects=True
        ),
    )(block_count, send, field, cot, rule, weight_one, weight_two)
    return output[None, None], grad_input[None, None], one, two


def solution(mesh):
    placed = (
        P("gx", "gy", None, None),
        P("gx", "gy", None, None),
        P(),
        P(),
        P("gx", "gy"),
        P("gx", "gy", None, None),
        P("gx", "gy", None, None),
    )
    return jax.shard_map(
        on_device,
        mesh=mesh,
        in_specs=placed,
        out_specs=(
            P("gx", "gy", None, None),
            P("gx", "gy", None, None),
            P(None, "gx", None),
            P(None, "gx", None),
        ),
        check_vma=False,
    )
```

```python
import functools

import jax
import jax.numpy as jnp
from jax import lax
from jax.experimental import pallas as pl
from jax.experimental.pallas import tpu as pltpu
from jax.sharding import PartitionSpec as P

BLK = 64
EARLY = 6
F32 = jnp.float32
BF16 = jnp.bfloat16
I16 = jnp.int16
MESH = pl.DeviceIdType.MESH
DIRECTIONS = ((-1, -1), (-1, 0), (-1, 1), (0, -1), (0, 1), (1, -1), (1, 0), (1, 1))

VM = pl.BlockSpec(memory_space=pltpu.VMEM)
SM = pl.BlockSpec(memory_space=pltpu.SMEM)
ANY = pl.BlockSpec(memory_space=pl.ANY)


def whole_kernel(
    nx, ny, groups, orders,
    count, send, features, cotangent, rule, w1_in, w2_in,
    output, grad_input, grad_one, grad_two,
    feat, cot, rule3, w1, w2, flat, low, packed, index, masks, columns,
    wide1, wide2, tall, field, hidden, upstream, grad, pre, gathered, buf, found, acc, own, sums,
    outs, backs, rets, gsend, prec, red, xrecv, ysend, yrecv,
    load_s, halo_ss, halo_rs, pss, prs, xss, xrs, yss, yrs,
):
    a, b = lax.axis_index("gx"), lax.axis_index("gy")
    nblk, blk, channels = field.shape
    rows = nblk * blk
    kernel = w1.shape[0]
    mid = kernel // 2
    per = send.shape[0]
    slot = per * blk
    chunk = channels // nx
    depth = acc.shape[0]
    first_slots = (depth - rows) // slot
    zero_row = rows + 8 * slot
    core = lax.rem(a, 2)
    chip = a // 2
    chips = nx // 2
    hops = ysend.shape[1]

    def exists(e):
        dx, dy = DIRECTIONS[e]
        x, y = a + dx, b + dy
        return (x >= 0) & (x < nx) & (y >= 0) & (y < ny)

    def place(e):
        dx, dy = DIRECTIONS[e]
        return (a + dx, b + dy)

    loads = [
        pltpu.make_async_copy(src, dst, load_s.at[n])
        for n, (src, dst) in enumerate((
            (features, feat), (rule, rule3), (cotangent, cot), (w2_in, w2), (w1_in, w1),
        ))
    ]
    for copy in loads:
        copy.start()

    barrier = pltpu.get_barrier_semaphore()
    for off in range(1, nx):
        pl.semaphore_signal(barrier, inc=1, device_id=(lax.rem(a + off, nx), b), device_id_type=MESH)
    for off in range(1, ny):
        pl.semaphore_signal(barrier, inc=1, device_id=(a, lax.rem(b + off, ny)), device_id_type=MESH)
    corners = (0, 2, 5, 7)
    for e in corners:
        dx, dy = DIRECTIONS[e]
        corner = (lax.rem(a + dx + nx, nx), lax.rem(b + dy + ny, ny))
        pl.semaphore_signal(barrier, inc=1, device_id=corner, device_id_type=MESH)

    def wide_view(wide, j):
        if j < first_slots:
            return wide.at[pl.ds(rows + j * slot, slot), pl.ds(0, channels)]
        return wide.at[pl.ds((j - first_slots) * slot, slot), pl.ds(channels, channels)]

    for j in range(8):
        @pl.when(jnp.logical_not(exists(j)))
        def _():
            blank = jnp.zeros((slot, channels), BF16)
            wide_view(wide1, j)[...] = blank
            wide_view(wide2, j)[...] = blank
            rets[0, j] = blank
            rets[1, j] = blank

    loads[0].wait()
    ids = lax.broadcasted_iota(jnp.int32, (rows, 1), 0)
    live = (ids < count[0, 0] * blk).astype(F32)
    masked32 = feat[...].astype(F32) * live
    masked = masked32.astype(BF16)
    field[...] = masked.reshape(nblk, blk, channels)
    wide1[:rows, :channels] = masked

    def ext_copy(x, e, wide):
        return pltpu.make_async_remote_copy(
            src_ref=outs.at[x, e], dst_ref=wide_view(wide, 7 - e),
            send_sem=halo_ss.at[x, e], recv_sem=halo_rs.at[x, 7 - e],
            device_id=place(e), device_id_type=MESH,
        )

    def back_copy(x, j):
        return pltpu.make_async_remote_copy(
            src_ref=backs.at[x, j], dst_ref=rets.at[x, j],
            send_sem=halo_ss.at[2 + x, j], recv_sem=halo_rs.at[2 + x, j],
            device_id=place(j), device_id_type=MESH,
        )

    def pack_ext(x, source):
        for e in range(8):
            for s in range(per):
                outs[x, e, s * blk : (s + 1) * blk, :] = source[send[s, e]]

    def start_ext(x, wide):
        for e in range(8):
            @pl.when(exists(e))
            def _():
                ext_copy(x, e, wide).start()

    def wait_ext(x, wide):
        for e in range(8):
            @pl.when(exists(7 - e))
            def _():
                ext_copy(x, e, wide).wait_recv()

    def fill_tall(wide):
        tall[:rows] = wide[:rows, :channels].astype(F32)
        for j in range(8):
            tall[rows + j * slot : rows + (j + 1) * slot] = wide_view(wide, j)[...].astype(F32)

    def send_back(x):
        for j in range(8):
            backs[x, j] = wide_view(acc, j)[...].astype(BF16)

            @pl.when(exists(j))
            def _():
                back_copy(x, j).start()

    def wait_back(x):
        for j in range(8):
            @pl.when(exists(7 - j))
            def _():
                back_copy(x, j).wait_recv()

    def returned_total(x):
        part = 32
        for h in range(0, blk, part):
            totals = [own[n * blk + h : n * blk + h + part, :] for n in range(nblk)]
            for e in range(8):
                for s in range(per):
                    value = rets[x, e, s * blk + h : s * blk + h + part, :].astype(F32)
                    target = send[s, 7 - e]
                    for n in range(nblk):
                        totals[n] += jnp.where(target == n, 1.0, 0.0) * value
            for n in range(nblk):
                own[n * blk + h : n * blk + h + part, :] = totals[n]

    pack_ext(0, field)
    pl.semaphore_wait(barrier, nx - 1 + ny - 1 + len(corners))
    start_ext(0, wide1)

    loads[1].wait()
    for k in range(kernel):
        flat[k : k + 1, :] = rule3[k]
    flat[kernel:, :] = jnp.full((flat.shape[0] - kernel, rows), zero_row, jnp.int32)
    book = flat[...]
    packed[...] = book[:, : rows // 2] + book[:, rows // 2 :] * 65536
    to_smem = pltpu.make_async_copy(packed, index, load_s.at[5])
    to_smem.start()
    second = book >= depth
    low[...] = jnp.where(second, book - depth, book)
    chosen = jnp.where(second, 1.0, 0.0).astype(BF16)
    within = jnp.where(second, book - depth, book)
    digits = jnp.concatenate([within // 256, lax.rem(within, 256)], axis=0).astype(F32).astype(BF16)
    shown = (flat.shape[0], 2 * channels)
    for s in range(mid):
        picks = jnp.where(
            lax.broadcasted_iota(jnp.int32, shown, 0)
            == jnp.where(lax.broadcasted_iota(jnp.int32, shown, 1) < channels, s, s + mid + 1),
            1.0, 0.0,
        ).astype(BF16)
        masks[s] = lax.dot_general(
            chosen, picks, (((0,), (0,)), ((), ())), preferred_element_type=F32
        ).astype(BF16)
        if s >= EARLY:
            weighted = jnp.concatenate([picks * 256.0, picks], axis=0)
            columns[s - EARLY] = lax.dot_general(
                digits, weighted, (((0,), (0,)), ((), ())), preferred_element_type=F32
            ).astype(jnp.int32).astype(I16)
    loads[2].wait()
    upstream[...] = (cot[...].astype(F32) * live).astype(BF16)
    tall[zero_row : zero_row + 8] = jnp.zeros((8, channels), F32)
    loads[3].wait()
    loads[4].wait()

    def pair(s):
        return (s, s + mid + 1)

    def stacked(w, s):
        return jnp.concatenate([w[k] for k in pair(s)], axis=0)

    def scatter(s, g, w):
        terms = lax.dot_general(
            g, stacked(w, s), (((1,), (1,)), ((), ())), preferred_element_type=F32
        ).astype(BF16)
        upper = terms * masks[s]
        lower = terms - upper
        values = jnp.concatenate(
            [
                jnp.concatenate(
                    [part[:, u * channels : (u + 1) * channels] for part in (lower, upper)], axis=1
                )
                for u in range(2)
            ],
            axis=0,
        )
        place_of = lax.broadcasted_iota(I16, (depth, rows), 0)
        hots = []
        for k in pair(s):
            wanted = jnp.broadcast_to(low[pl.ds(k, 1), :].astype(I16), (depth, rows))
            hots.append(jnp.where(place_of == wanted, jnp.ones((), BF16), jnp.zeros((), BF16)))
        acc[...] += jnp.dot(jnp.concatenate(hots, axis=1), values, preferred_element_type=F32)

    def scatter_first(g, w):
        acc[...] = jnp.zeros_like(acc)
        acc[:rows, :channels] = lax.dot_general(
            g, w[mid], (((1,), (1,)), ((), ())), preferred_element_type=F32
        )

    def gather(s):
        for u, k in enumerate(pair(s)):
            for n in range(rows // 2):
                word = index[k, n]
                buf[u, n : n + 1, :] = tall[pl.ds(jnp.bitwise_and(word, 65535), 1), :]
                other = n + rows // 2
                buf[u, other : other + 1, :] = tall[pl.ds(lax.shift_right_logical(word, 16), 1), :]

    def gather_dots(s, wide):
        lanes = lax.broadcasted_iota(I16, (rows, channels), 1)
        hots = []
        for u in range(2):
            wanted = columns[s - EARLY, :, u * channels : (u + 1) * channels]
            hots.append(jnp.concatenate(
                [
                    jnp.where(wanted == lanes + I16(t * channels), jnp.ones((), BF16), jnp.zeros((), BF16))
                    for t in range(depth // channels)
                ],
                axis=1,
            ))
        sums_of = jnp.dot(jnp.concatenate(hots, axis=0), wide[...], preferred_element_type=F32)
        for u in range(2):
            upper = masks[s, :, u * channels : (u + 1) * channels].astype(F32) > 0.5
            part = sums_of[u * rows : (u + 1) * rows]
            found[:, u * channels : (u + 1) * channels] = jnp.where(
                upper, part[:, channels:], part[:, :channels]
            ).astype(BF16)

    def clear():
        buf[...] = jnp.zeros_like(buf)
        found[...] = jnp.zeros_like(found)

    def keep(s, picks):
        for u, k in enumerate(pair(s)):
            gathered[k] = picks[:, u * channels : (u + 1) * channels]
        return picks

    def settle(s):
        return keep(s, jnp.concatenate([buf[0].astype(BF16), buf[1].astype(BF16)], axis=1))

    def settle_dots(s):
        return keep(s, found[...])

    def both(s):
        return jnp.concatenate([gathered[k] for k in pair(s)], axis=1)

    def keep_partial(g, at, picks, rows_out):
        part = lax.dot_general(
            picks, rows_out, (((0,), (0,)), ((), ())), preferred_element_type=F32
        ).astype(BF16)
        for u in range(2):
            for p in range(nx):
                first = u * channels + p * chunk
                gsend[g, p % 2, p // 2, 1 + 2 * at + u] = part[first : first + chunk, :]

    def keep_first(g, rows_in, rows_out):
        part = lax.dot_general(
            rows_in, rows_out, (((0,), (0,)), ((), ())), preferred_element_type=F32
        ).astype(BF16)
        for p in range(nx):
            gsend[g, p % 2, p // 2, 0] = part[p * chunk : (p + 1) * chunk, :]

    def span(t):
        g, first, last = groups[t]
        return g, pl.ds(first, last - first)

    def pair_copy(t):
        g, qs = span(t)
        return pltpu.make_async_remote_copy(
            src_ref=gsend.at[g, 1 - core, :, qs], dst_ref=prec.at[g, :, qs],
            send_sem=pss.at[t], recv_sem=prs.at[t],
            device_id=(a + 1 - 2 * core, b), device_id_type=MESH,
        )

    def chip_copy(t, off):
        g, qs = span(t)
        peer = lax.rem(chip + off, chips)
        return pltpu.make_async_remote_copy(
            src_ref=red.at[g, peer, qs], dst_ref=xrecv.at[g, off, qs],
            send_sem=xss.at[t, off], recv_sem=xrs.at[t, off],
            device_id=(2 * peer + core, b), device_id_type=MESH,
        )

    def gy_copy(t, n):
        g, qs = span(t)
        step = 1 << n
        return pltpu.make_async_remote_copy(
            src_ref=ysend.at[g, n, qs], dst_ref=yrecv.at[g, n, qs],
            send_sem=yss.at[t, n], recv_sem=yrs.at[t, n],
            device_id=(a, b + step * (1 - 2 * lax.rem(b // step, 2))), device_id_type=MESH,
        )

    def reduce_pair(t):
        g, qs = span(t)
        pair_copy(t).wait_recv()
        for n in range(chips):
            red[g, n, qs] = (gsend[g, core, n, qs].astype(F32) + prec[g, n, qs].astype(F32)).astype(BF16)
        for off in range(1, chips):
            chip_copy(t, off).start()

    def reduce_chips(t):
        g, qs = span(t)
        total = red[g, chip, qs].astype(F32)
        for off in range(1, chips):
            chip_copy(t, off).wait_recv()
            total += xrecv[g, off, qs].astype(F32)
        ysend[g, 0, qs] = total.astype(BF16)
        gy_copy(t, 0).start()

    def reduce_gy(t, n):
        g, first, last = groups[t]
        _, qs = span(t)
        gy_copy(t, n).wait_recv()
        total = ysend[g, n, qs].astype(F32) + yrecv[g, n, qs].astype(F32)
        if n + 1 < hops:
            ysend[g, n + 1, qs] = total.astype(BF16)
            gy_copy(t, n + 1).start()
            return
        total = total * (1.0 / (nx * ny))
        out = (grad_one, grad_two)[g]
        for q in range(first, last):
            k = mid if q == 0 else orders[g][(q - 1) // 2] + ((q - 1) % 2) * (mid + 1)
            out[k] = total[q - first]

    scatter_first(upstream[...], w2)

    @pl.loop(0, EARLY // 2)
    def _(s):
        scatter(2 * s, upstream[...], w2)
        scatter(2 * s + 1, upstream[...], w2)

    clear()
    wait_ext(0, wide1)
    fill_tall(wide1)
    to_smem.wait()
    pre[...] = jnp.dot(wide1[:rows, :channels], w1[mid], preferred_element_type=F32)

    def first_conv(s, picks):
        pre[...] += jnp.dot(picks, stacked(w1, s), preferred_element_type=F32)

    beside = mid - EARLY
    rest = EARLY // 2

    @pl.loop(0, beside)
    def _(s):
        last = jnp.where(s == 0, mid - rest - 1, s - 1)
        first_conv(last, settle(last))
        scatter(s + EARLY, upstream[...], w2)
        gather(s)

    send_back(0)
    own[...] = acc[:rows, :channels]

    @pl.loop(0, rest)
    def _(c):
        last = beside - 1 + c
        first_conv(last, settle(last))
        last = jnp.where(c == 0, mid - 1, mid - rest - 1 + c)
        first_conv(last, settle_dots(last))
        gather_dots(mid - rest + c, wide1)
        gather(beside + c)

    for last, picks in ((mid - rest - 1, settle), (mid - 1, settle_dots)):
        first_conv(last, picks(last))
    v = pre[...] * live
    pre[...] = v
    hid = (v / (1.0 + jnp.exp(-v))).astype(BF16)
    hidden[...] = hid.reshape(nblk, blk, channels)
    wide2[:rows, :channels] = hid
    pack_ext(1, hidden)
    start_ext(1, wide2)

    wait_back(0)
    returned_total(0)
    v = pre[...]
    s = 1.0 / (1.0 + jnp.exp(-v))
    grad[...] = (own[...] * s * (1.0 + v * (1.0 - s)) * live).astype(BF16)

    keep_first(0, wide1[:rows, :channels], grad[...])
    for s in range(4 * (EARLY // 2), mid):
        keep_partial(0, s, both(s), grad[...])
    scatter_first(grad[...], w1)

    @pl.loop(0, EARLY // 2)
    def _(s):
        scatter(s, grad[...], w1)
        for n in range(4):
            keep_partial(0, 4 * s + n, both(4 * s + n), grad[...])

    pair_copy(0).start()

    @pl.loop(EARLY // 2, EARLY)
    def _(s):
        scatter(s, grad[...], w1)

    reduce_pair(0)
    clear()
    wait_ext(1, wide2)
    fill_tall(wide2)
    sums[...] = jnp.dot(wide2[:rows, :channels], w2[mid], preferred_element_type=F32)
    keep_first(1, wide2[:rows, :channels], upstream[...])

    def second_conv(s, picks):
        sums[...] += jnp.dot(picks, stacked(w2, s), preferred_element_type=F32)

    def keep_group(t):
        for at, s in enumerate(orders[1]):
            if groups[t][1] <= 1 + 2 * at < groups[t][2]:
                keep_partial(1, at, both(s), upstream[...])
        pair_copy(t).start()

    @pl.loop(0, EARLY)
    def _(c):
        @pl.when(c == rest + 1)
        def _():
            keep_group(1)
            reduce_chips(0)

        @pl.when(c == EARLY - 1)
        def _():
            reduce_pair(1)

        last = jnp.where(c == 0, EARLY - 1, c - 1)
        second_conv(last, settle(last))
        last = jnp.where(c == 0, mid - 2, EARLY - 1 + c)
        second_conv(last, settle_dots(last))
        gather_dots(EARLY + c, wide2)
        gather(c)

    second_conv(EARLY - 1, settle(EARLY - 1))
    second_conv(mid - 2, settle_dots(mid - 2))
    gather_dots(mid - 1, wide2)
    second_conv(mid - 1, settle_dots(mid - 1))
    keep_group(2)
    reduce_gy(0, 0)
    output[...] = (sums[...] * live).astype(BF16)

    def scatters(first, last):
        @pl.loop(0, (last - first) // 2)
        def _(n):
            scatter(first + 2 * n, grad[...], w1)
            scatter(first + 2 * n + 1, grad[...], w1)

    scatter(EARLY, grad[...], w1)
    reduce_pair(2)
    reduce_chips(1)
    scatters(EARLY + 1, mid - 2)
    reduce_gy(1, 0)
    reduce_chips(2)
    scatters(mid - 2, mid)
    send_back(1)
    own[...] = acc[:rows, :channels]
    for n in range(hops):
        for t in range(len(groups)):
            if n > 0 or t > 1:
                reduce_gy(t, n)
    wait_back(1)
    returned_total(1)
    grad_input[...] = (own[...] * live).astype(BF16)

    for e in range(8):
        @pl.when(exists(e))
        def _():
            ext_copy(0, e, wide1).wait_send()
            ext_copy(1, e, wide2).wait_send()
            back_copy(0, e).wait_send()
            back_copy(1, e).wait_send()
    for t in range(len(groups)):
        pair_copy(t).wait_send()
        for off in range(1, chips):
            chip_copy(t, off).wait_send()
        for n in range(hops):
            gy_copy(t, n).wait_send()


def move_kernel(*refs):
    for n in range(4):
        refs[4 + n][...] = refs[n][...]


def on_device(features, cotangent, weight_one, weight_two, block_count, send_list, rulebook):
    field, cot = features[0, 0], cotangent[0, 0]
    rows, channels = field.shape
    kernel = rulebook.shape[2]
    mid = kernel // 2
    send = send_list[0, 0].T
    rule = rulebook.reshape(kernel, 1, rows)
    slot = send.shape[0] * BLK
    nx, ny = lax.axis_size("gx"), lax.axis_size("gy")
    chunk = channels // nx
    depth = (rows + 8 * slot) // 2
    tall_rows = rows + 8 * slot + 8
    rest = EARLY // 2
    early = [n + c for n in (0, EARLY) for c in range(rest)]
    order = early + [s for s in range(mid) if s not in early]
    orders = (tuple(range(mid)), tuple(order))
    groups = ((0, 0, kernel), (1, 0, 1 + 2 * len(early)), (1, 1 + 2 * len(early), kernel))
    hops = (ny - 1).bit_length()
    shape = jax.ShapeDtypeStruct
    grads = shape((kernel, chunk, channels), F32)
    plain_f = pltpu.VMEM((rows, channels), F32)
    plain_b = pltpu.VMEM((rows, channels), BF16)
    blocks = pltpu.VMEM((rows // BLK, BLK, channels), BF16)
    halos = pltpu.VMEM((2, 8, slot, channels), BF16)
    wide = pltpu.VMEM((depth, 2 * channels), BF16)
    weights = pltpu.VMEM((kernel, channels, channels), BF16)
    high = -(-kernel // 8) * 8
    parts = len(groups)
    tile = (chunk, channels)
    sem = pltpu.SemaphoreType.DMA
    output, grad_input, one, two = pl.pallas_call(
        functools.partial(whole_kernel, nx, ny, groups, orders),
        out_shape=(shape((rows, channels), BF16),) * 2 + (grads, grads),
        in_specs=[SM, SM] + [ANY] * 5,
        out_specs=(VM,) * 4,
        scratch_shapes=[
            plain_b, plain_b, pltpu.VMEM((kernel, 1, rows), jnp.int32), weights, weights,
            pltpu.VMEM((high, rows), jnp.int32), pltpu.VMEM((high, rows), jnp.int32),
            pltpu.VMEM((high, rows // 2), jnp.int32), pltpu.SMEM((high, rows // 2), jnp.int32),
            pltpu.VMEM((mid, rows, 2 * channels), BF16),
            pltpu.VMEM((mid - EARLY, rows, 2 * channels), I16),
            wide, wide, pltpu.VMEM((tall_rows, channels), F32), blocks, blocks,
            plain_b, plain_b, plain_f, pltpu.VMEM((kernel, rows, channels), BF16),
            pltpu.VMEM((2, rows, channels), F32), pltpu.VMEM((rows, 2 * channels), BF16),
            pltpu.VMEM((depth, 2 * channels), F32),
            plain_f, plain_f, halos, halos, halos,
            pltpu.VMEM((2, 2, nx // 2, kernel) + tile, BF16),
            pltpu.VMEM((2, nx // 2, kernel) + tile, BF16),
            pltpu.VMEM((2, nx // 2, kernel) + tile, BF16),
            pltpu.VMEM((2, nx // 2, kernel) + tile, BF16),
            pltpu.VMEM((2, hops, kernel) + tile, BF16),
            pltpu.VMEM((2, hops, kernel) + tile, BF16),
            sem((6,)), sem((4, 8)), sem((4, 8)), sem((parts,)), sem((parts,)),
            sem((parts, nx // 2)), sem((parts, nx // 2)), sem((parts, hops)), sem((parts, hops)),
        ],
        compiler_params=pltpu.CompilerParams(
            vmem_limit_bytes=56 << 20, collective_id=0, has_side_effects=True
        ),
    )(block_count, send, field, cot, rule, weight_one, weight_two)
    results = (output, grad_input, one, two)
    output, grad_input, one, two = pl.pallas_call(
        move_kernel,
        out_shape=tuple(shape(x.shape, x.dtype) for x in results),
        in_specs=[VM] * 4,
        out_specs=(VM,) * 4,
    )(*results)
    return output[None, None], grad_input[None, None], one, two


def solution(mesh):
    placed = (
        P("gx", "gy", None, None),
        P("gx", "gy", None, None),
        P(),
        P(),
        P("gx", "gy"),
        P("gx", "gy", None, None),
        P("gx", "gy", None, None),
    )
    return jax.shard_map(
        on_device,
        mesh=mesh,
        in_specs=placed,
        out_specs=(
            P("gx", "gy", None, None),
            P("gx", "gy", None, None),
            P(None, "gx", None),
            P(None, "gx", None),
        ),
        check_vma=False,
    )
```

```python
import functools

import jax
import jax.numpy as jnp
from jax import lax
from jax.experimental import pallas as pl
from jax.experimental.pallas import tpu as pltpu
from jax.sharding import PartitionSpec as P

BLK = 64
EARLY = 6
F32 = jnp.float32
BF16 = jnp.bfloat16
I16 = jnp.int16
MESH = pl.DeviceIdType.MESH
DIRECTIONS = ((-1, -1), (-1, 0), (-1, 1), (0, -1), (0, 1), (1, -1), (1, 0), (1, 1))

VM = pl.BlockSpec(memory_space=pltpu.VMEM)
SM = pl.BlockSpec(memory_space=pltpu.SMEM)
ANY = pl.BlockSpec(memory_space=pl.ANY)


def whole_kernel(
    nx, ny, groups,
    count, send, features, cotangent, rule, w1_in, w2_in,
    output, grad_input, grad_one, grad_two,
    feat, cot, rule3, w1, w2, flat, low, masks, columns,
    wide1, wide2, field, hidden, upstream, grad, pre, gathered, found, acc, own, sums,
    outs, backs, rets, gsend, prec, red, xrecv, ysend, yrecv,
    load_s, halo_ss, halo_rs, pss, prs, xss, xrs, yss, yrs,
):
    a, b = lax.axis_index("gx"), lax.axis_index("gy")
    nblk, blk, channels = field.shape
    rows = nblk * blk
    kernel = w1.shape[0]
    mid = kernel // 2
    per = send.shape[0]
    slot = per * blk
    chunk = channels // nx
    depth = acc.shape[0]
    first_slots = (depth - rows) // slot
    zero_row = rows + 8 * slot
    core = lax.rem(a, 2)
    chip = a // 2
    chips = nx // 2
    hops = ysend.shape[1]

    def exists(e):
        dx, dy = DIRECTIONS[e]
        x, y = a + dx, b + dy
        return (x >= 0) & (x < nx) & (y >= 0) & (y < ny)

    def place(e):
        dx, dy = DIRECTIONS[e]
        return (a + dx, b + dy)

    loads = [
        pltpu.make_async_copy(src, dst, load_s.at[n])
        for n, (src, dst) in enumerate((
            (features, feat), (rule, rule3), (cotangent, cot), (w2_in, w2), (w1_in, w1),
        ))
    ]
    for copy in loads:
        copy.start()

    barrier = pltpu.get_barrier_semaphore()
    for off in range(1, nx):
        pl.semaphore_signal(barrier, inc=1, device_id=(lax.rem(a + off, nx), b), device_id_type=MESH)
    for off in range(1, ny):
        pl.semaphore_signal(barrier, inc=1, device_id=(a, lax.rem(b + off, ny)), device_id_type=MESH)
    corners = (0, 2, 5, 7)
    for e in corners:
        dx, dy = DIRECTIONS[e]
        corner = (lax.rem(a + dx + nx, nx), lax.rem(b + dy + ny, ny))
        pl.semaphore_signal(barrier, inc=1, device_id=corner, device_id_type=MESH)

    def wide_view(wide, j):
        if j < first_slots:
            return wide.at[pl.ds(rows + j * slot, slot), pl.ds(0, channels)]
        return wide.at[pl.ds((j - first_slots) * slot, slot), pl.ds(channels, channels)]

    for j in range(8):
        @pl.when(jnp.logical_not(exists(j)))
        def _():
            blank = jnp.zeros((slot, channels), BF16)
            wide_view(wide1, j)[...] = blank
            wide_view(wide2, j)[...] = blank
            rets[0, j] = blank
            rets[1, j] = blank

    loads[0].wait()
    ids = lax.broadcasted_iota(jnp.int32, (rows, 1), 0)
    live = (ids < count[0, 0] * blk).astype(F32)
    masked32 = feat[...].astype(F32) * live
    masked = masked32.astype(BF16)
    field[...] = masked.reshape(nblk, blk, channels)
    wide1[:rows, :channels] = masked

    def ext_copy(x, e, wide):
        return pltpu.make_async_remote_copy(
            src_ref=outs.at[x, e], dst_ref=wide_view(wide, 7 - e),
            send_sem=halo_ss.at[x, e], recv_sem=halo_rs.at[x, 7 - e],
            device_id=place(e), device_id_type=MESH,
        )

    def back_copy(x, j):
        return pltpu.make_async_remote_copy(
            src_ref=backs.at[x, j], dst_ref=rets.at[x, j],
            send_sem=halo_ss.at[2 + x, j], recv_sem=halo_rs.at[2 + x, j],
            device_id=place(j), device_id_type=MESH,
        )

    def pack_ext(x, source):
        for e in range(8):
            for s in range(per):
                outs[x, e, s * blk : (s + 1) * blk, :] = source[send[s, e]]

    def start_ext(x, wide):
        for e in range(8):
            @pl.when(exists(e))
            def _():
                ext_copy(x, e, wide).start()

    def wait_ext(x, wide):
        for e in range(8):
            @pl.when(exists(7 - e))
            def _():
                ext_copy(x, e, wide).wait_recv()

    def send_back(x):
        for j in range(8):
            backs[x, j] = wide_view(acc, j)[...].astype(BF16)

            @pl.when(exists(j))
            def _():
                back_copy(x, j).start()

    def wait_back(x):
        for j in range(8):
            @pl.when(exists(7 - j))
            def _():
                back_copy(x, j).wait_recv()

    def returned_total(x):
        part = 32
        for h in range(0, blk, part):
            totals = [own[n * blk + h : n * blk + h + part, :] for n in range(nblk)]
            for e in range(8):
                for s in range(per):
                    value = rets[x, e, s * blk + h : s * blk + h + part, :].astype(F32)
                    target = send[s, 7 - e]
                    for n in range(nblk):
                        totals[n] += jnp.where(target == n, 1.0, 0.0) * value
            for n in range(nblk):
                own[n * blk + h : n * blk + h + part, :] = totals[n]

    pack_ext(0, field)
    pl.semaphore_wait(barrier, nx - 1 + ny - 1 + len(corners))
    start_ext(0, wide1)

    loads[1].wait()
    for k in range(kernel):
        flat[k : k + 1, :] = rule3[k]
    flat[kernel:, :] = jnp.full((flat.shape[0] - kernel, rows), zero_row, jnp.int32)
    book = flat[...]
    second = book >= depth
    low[...] = jnp.where(second, book - depth, book)
    chosen = jnp.where(second, 1.0, 0.0).astype(BF16)
    within = jnp.where(second, book - depth, book)
    digits = jnp.concatenate([within // 256, lax.rem(within, 256)], axis=0).astype(F32).astype(BF16)
    shown = (flat.shape[0], 2 * channels)
    lanes_of = lax.broadcasted_iota(jnp.int32, shown, 1)
    rows_of = lax.broadcasted_iota(jnp.int32, shown, 0)

    @pl.loop(0, mid)
    def _(s):
        offset = jnp.where(lanes_of < channels, s, s + mid + 1)
        picks = jnp.where(rows_of == offset, 1.0, 0.0).astype(BF16)
        masks[s] = lax.dot_general(
            chosen, picks, (((0,), (0,)), ((), ())), preferred_element_type=F32
        ).astype(BF16)
        weighted = jnp.concatenate([picks * 256.0, picks], axis=0)
        columns[s] = lax.dot_general(
            digits, weighted, (((0,), (0,)), ((), ())), preferred_element_type=F32
        ).astype(jnp.int32).astype(I16)

    loads[2].wait()
    upstream[...] = (cot[...].astype(F32) * live).astype(BF16)
    loads[3].wait()
    loads[4].wait()

    def pair(s):
        return (s, s + mid + 1)

    def stacked(w, s):
        return jnp.concatenate([w[k] for k in pair(s)], axis=0)

    def scatter(s, g, w):
        terms = lax.dot_general(
            g, stacked(w, s), (((1,), (1,)), ((), ())), preferred_element_type=F32
        ).astype(BF16)
        upper = terms * masks[s]
        lower = terms - upper
        values = jnp.concatenate(
            [
                jnp.concatenate(
                    [part[:, u * channels : (u + 1) * channels] for part in (lower, upper)], axis=1
                )
                for u in range(2)
            ],
            axis=0,
        )
        place_of = lax.broadcasted_iota(I16, (depth, rows), 0)
        hots = []
        for k in pair(s):
            wanted = jnp.broadcast_to(low[pl.ds(k, 1), :].astype(I16), (depth, rows))
            hots.append(jnp.where(place_of == wanted, jnp.ones((), BF16), jnp.zeros((), BF16)))
        acc[...] += jnp.dot(jnp.concatenate(hots, axis=1), values, preferred_element_type=F32)

    def scatter_first(g, w):
        acc[...] = jnp.zeros_like(acc)
        acc[:rows, :channels] = lax.dot_general(
            g, w[mid], (((1,), (1,)), ((), ())), preferred_element_type=F32
        )

    def gather_dots(s, wide):
        lanes = lax.broadcasted_iota(I16, (rows, channels), 1)
        hots = []
        for u in range(2):
            wanted = columns[s, :, u * channels : (u + 1) * channels]
            hots.append(jnp.concatenate(
                [
                    jnp.where(wanted == lanes + I16(t * channels), jnp.ones((), BF16), jnp.zeros((), BF16))
                    for t in range(depth // channels)
                ],
                axis=1,
            ))
        sums_of = jnp.dot(jnp.concatenate(hots, axis=0), wide[...], preferred_element_type=F32)
        for u in range(2):
            upper = masks[s, :, u * channels : (u + 1) * channels].astype(F32) > 0.5
            part = sums_of[u * rows : (u + 1) * rows]
            found[:, u * channels : (u + 1) * channels] = jnp.where(
                upper, part[:, channels:], part[:, :channels]
            ).astype(BF16)

    def clear():
        found[...] = jnp.zeros_like(found)

    def keep(s, picks):
        for u, k in enumerate(pair(s)):
            gathered[k] = picks[:, u * channels : (u + 1) * channels]
        return picks

    def settle_dots(s):
        return keep(s, found[...])

    def both(s):
        return jnp.concatenate([gathered[k] for k in pair(s)], axis=1)

    def keep_partial(g, at, picks, rows_out):
        part = lax.dot_general(
            picks, rows_out, (((0,), (0,)), ((), ())), preferred_element_type=F32
        ).astype(BF16)
        for u in range(2):
            for p in range(nx):
                first = u * channels + p * chunk
                gsend[g, p % 2, p // 2, 1 + 2 * at + u] = part[first : first + chunk, :]

    def keep_first(g, rows_in, rows_out):
        part = lax.dot_general(
            rows_in, rows_out, (((0,), (0,)), ((), ())), preferred_element_type=F32
        ).astype(BF16)
        for p in range(nx):
            gsend[g, p % 2, p // 2, 0] = part[p * chunk : (p + 1) * chunk, :]

    def span(t):
        g, first, last = groups[t]
        return g, pl.ds(first, last - first)

    def pair_copy(t):
        g, qs = span(t)
        return pltpu.make_async_remote_copy(
            src_ref=gsend.at[g, 1 - core, :, qs], dst_ref=prec.at[g, :, qs],
            send_sem=pss.at[t], recv_sem=prs.at[t],
            device_id=(a + 1 - 2 * core, b), device_id_type=MESH,
        )

    def chip_copy(t, off):
        g, qs = span(t)
        peer = lax.rem(chip + off, chips)
        return pltpu.make_async_remote_copy(
            src_ref=red.at[g, peer, qs], dst_ref=xrecv.at[g, off, qs],
            send_sem=xss.at[t, off], recv_sem=xrs.at[t, off],
            device_id=(2 * peer + core, b), device_id_type=MESH,
        )

    def gy_copy(t, n):
        g, qs = span(t)
        step = 1 << n
        return pltpu.make_async_remote_copy(
            src_ref=ysend.at[g, n, qs], dst_ref=yrecv.at[g, n, qs],
            send_sem=yss.at[t, n], recv_sem=yrs.at[t, n],
            device_id=(a, b + step * (1 - 2 * lax.rem(b // step, 2))), device_id_type=MESH,
        )

    def reduce_pair(t):
        g, qs = span(t)
        pair_copy(t).wait_recv()
        for n in range(chips):
            red[g, n, qs] = (gsend[g, core, n, qs].astype(F32) + prec[g, n, qs].astype(F32)).astype(BF16)
        for off in range(1, chips):
            chip_copy(t, off).start()

    def reduce_chips(t):
        g, qs = span(t)
        total = red[g, chip, qs].astype(F32)
        for off in range(1, chips):
            chip_copy(t, off).wait_recv()
            total += xrecv[g, off, qs].astype(F32)
        ysend[g, 0, qs] = total.astype(BF16)
        gy_copy(t, 0).start()

    def reduce_gy(t, n):
        g, first, last = groups[t]
        _, qs = span(t)
        gy_copy(t, n).wait_recv()
        total = ysend[g, n, qs].astype(F32) + yrecv[g, n, qs].astype(F32)
        if n + 1 < hops:
            ysend[g, n + 1, qs] = total.astype(BF16)
            gy_copy(t, n + 1).start()
            return
        total = total * (1.0 / (nx * ny))
        out = (grad_one, grad_two)[g]
        for q in range(first, last):
            k = mid if q == 0 else (q - 1) // 2 + ((q - 1) % 2) * (mid + 1)
            out[k] = total[q - first]

    scatter_first(upstream[...], w2)

    @pl.loop(0, EARLY)
    def _(s):
        scatter(s, upstream[...], w2)

    clear()
    wait_ext(0, wide1)
    pre[...] = jnp.dot(wide1[:rows, :channels], w1[mid], preferred_element_type=F32)

    def first_conv(s, picks):
        pre[...] += jnp.dot(picks, stacked(w1, s), preferred_element_type=F32)

    beside = mid - EARLY

    def before(s):
        return jnp.where(s == 0, mid - 1, s - 1)

    @pl.loop(0, beside)
    def _(s):
        first_conv(before(s), settle_dots(before(s)))
        scatter(s + EARLY, upstream[...], w2)
        gather_dots(s, wide1)

    send_back(0)
    own[...] = acc[:rows, :channels]

    @pl.loop(beside, mid)
    def _(s):
        first_conv(s - 1, settle_dots(s - 1))
        gather_dots(s, wide1)

    first_conv(mid - 1, settle_dots(mid - 1))
    v = pre[...] * live
    pre[...] = v
    hid = (v / (1.0 + jnp.exp(-v))).astype(BF16)
    hidden[...] = hid.reshape(nblk, blk, channels)
    wide2[:rows, :channels] = hid
    pack_ext(1, hidden)
    start_ext(1, wide2)

    wait_back(0)
    returned_total(0)
    v = pre[...]
    s = 1.0 / (1.0 + jnp.exp(-v))
    grad[...] = (own[...] * s * (1.0 + v * (1.0 - s)) * live).astype(BF16)

    keep_first(0, wide1[:rows, :channels], grad[...])
    keep_partial(0, mid - 1, both(mid - 1), grad[...])
    scatter_first(grad[...], w1)

    @pl.loop(0, EARLY)
    def _(s):
        scatter(s, grad[...], w1)
        for n in range(2):
            keep_partial(0, 2 * s + n, both(2 * s + n), grad[...])

    pair_copy(0).start()
    clear()
    wait_ext(1, wide2)
    sums[...] = jnp.dot(wide2[:rows, :channels], w2[mid], preferred_element_type=F32)
    keep_first(1, wide2[:rows, :channels], upstream[...])

    def second_conv(s):
        picks = settle_dots(s)
        sums[...] += jnp.dot(picks, stacked(w2, s), preferred_element_type=F32)
        keep_partial(1, s, picks, upstream[...])

    @pl.loop(0, mid)
    def _(s):
        @pl.when(s == 2)
        def _():
            reduce_pair(0)

        @pl.when(s == beside + 1)
        def _():
            pair_copy(1).start()

        @pl.when(s == beside + 3)
        def _():
            reduce_pair(1)
            reduce_chips(0)

        second_conv(before(s))
        gather_dots(s, wide2)

    second_conv(mid - 1)
    pair_copy(2).start()
    reduce_gy(0, 0)
    output[...] = (sums[...] * live).astype(BF16)

    @pl.loop(EARLY, mid)
    def _(s):
        @pl.when(s == EARLY + 2)
        def _():
            reduce_pair(2)
            reduce_chips(1)

        @pl.when(s == EARLY + 5)
        def _():
            reduce_gy(1, 0)
            reduce_chips(2)

        scatter(s, grad[...], w1)

    send_back(1)
    own[...] = acc[:rows, :channels]
    for n in range(hops):
        for t in range(len(groups)):
            if n > 0 or t > 1:
                reduce_gy(t, n)
    wait_back(1)
    returned_total(1)
    grad_input[...] = (own[...] * live).astype(BF16)

    for e in range(8):
        @pl.when(exists(e))
        def _():
            ext_copy(0, e, wide1).wait_send()
            ext_copy(1, e, wide2).wait_send()
            back_copy(0, e).wait_send()
            back_copy(1, e).wait_send()
    for t in range(len(groups)):
        pair_copy(t).wait_send()
        for off in range(1, chips):
            chip_copy(t, off).wait_send()
        for n in range(hops):
            gy_copy(t, n).wait_send()


def move_kernel(*refs):
    for n in range(4):
        refs[4 + n][...] = refs[n][...]


def on_device(features, cotangent, weight_one, weight_two, block_count, send_list, rulebook):
    field, cot = features[0, 0], cotangent[0, 0]
    rows, channels = field.shape
    kernel = rulebook.shape[2]
    mid = kernel // 2
    send = send_list[0, 0].T
    rule = rulebook.reshape(kernel, 1, rows)
    slot = send.shape[0] * BLK
    nx, ny = lax.axis_size("gx"), lax.axis_size("gy")
    chunk = channels // nx
    depth = (rows + 8 * slot) // 2
    split = 1 + 2 * (mid - EARLY)
    groups = ((0, 0, kernel), (1, 0, split), (1, split, kernel))
    hops = (ny - 1).bit_length()
    shape = jax.ShapeDtypeStruct
    grads = shape((kernel, chunk, channels), F32)
    plain_f = pltpu.VMEM((rows, channels), F32)
    plain_b = pltpu.VMEM((rows, channels), BF16)
    blocks = pltpu.VMEM((rows // BLK, BLK, channels), BF16)
    halos = pltpu.VMEM((2, 8, slot, channels), BF16)
    wide = pltpu.VMEM((depth, 2 * channels), BF16)
    weights = pltpu.VMEM((kernel, channels, channels), BF16)
    high = -(-kernel // 8) * 8
    parts = len(groups)
    tile = (chunk, channels)
    sem = pltpu.SemaphoreType.DMA
    output, grad_input, one, two = pl.pallas_call(
        functools.partial(whole_kernel, nx, ny, groups),
        out_shape=(shape((rows, channels), BF16),) * 2 + (grads, grads),
        in_specs=[SM, SM] + [ANY] * 5,
        out_specs=(VM,) * 4,
        scratch_shapes=[
            plain_b, plain_b, pltpu.VMEM((kernel, 1, rows), jnp.int32), weights, weights,
            pltpu.VMEM((high, rows), jnp.int32), pltpu.VMEM((high, rows), jnp.int32),
            pltpu.VMEM((mid, rows, 2 * channels), BF16),
            pltpu.VMEM((mid, rows, 2 * channels), I16),
            wide, wide, blocks, blocks,
            plain_b, plain_b, plain_f, pltpu.VMEM((kernel, rows, channels), BF16),
            pltpu.VMEM((rows, 2 * channels), BF16),
            pltpu.VMEM((depth, 2 * channels), F32),
            plain_f, plain_f, halos, halos, halos,
            pltpu.VMEM((2, 2, nx // 2, kernel) + tile, BF16),
            pltpu.VMEM((2, nx // 2, kernel) + tile, BF16),
            pltpu.VMEM((2, nx // 2, kernel) + tile, BF16),
            pltpu.VMEM((2, nx // 2, kernel) + tile, BF16),
            pltpu.VMEM((2, hops, kernel) + tile, BF16),
            pltpu.VMEM((2, hops, kernel) + tile, BF16),
            sem((6,)), sem((4, 8)), sem((4, 8)), sem((parts,)), sem((parts,)),
            sem((parts, nx // 2)), sem((parts, nx // 2)), sem((parts, hops)), sem((parts, hops)),
        ],
        compiler_params=pltpu.CompilerParams(
            vmem_limit_bytes=56 << 20, collective_id=0, has_side_effects=True
        ),
    )(block_count, send, field, cot, rule, weight_one, weight_two)
    results = (output, grad_input, one, two)
    output, grad_input, one, two = pl.pallas_call(
        move_kernel,
        out_shape=tuple(shape(x.shape, x.dtype) for x in results),
        in_specs=[VM] * 4,
        out_specs=(VM,) * 4,
    )(*results)
    return output[None, None], grad_input[None, None], one, two


def solution(mesh):
    placed = (
        P("gx", "gy", None, None),
        P("gx", "gy", None, None),
        P(),
        P(),
        P("gx", "gy"),
        P("gx", "gy", None, None),
        P("gx", "gy", None, None),
    )
    return jax.shard_map(
        on_device,
        mesh=mesh,
        in_specs=placed,
        out_specs=(
            P("gx", "gy", None, None),
            P("gx", "gy", None, None),
            P(None, "gx", None),
            P(None, "gx", None),
        ),
        check_vma=False,
    )
```

```python
import functools

import jax
import jax.numpy as jnp
from jax import lax
from jax.experimental import pallas as pl
from jax.experimental.pallas import tpu as pltpu
from jax.sharding import PartitionSpec as P

BLK = 64
EARLY = 6
F32 = jnp.float32
BF16 = jnp.bfloat16
I16 = jnp.int16
MESH = pl.DeviceIdType.MESH
DIRECTIONS = ((-1, -1), (-1, 0), (-1, 1), (0, -1), (0, 1), (1, -1), (1, 0), (1, 1))

VM = pl.BlockSpec(memory_space=pltpu.VMEM)
SM = pl.BlockSpec(memory_space=pltpu.SMEM)
ANY = pl.BlockSpec(memory_space=pl.ANY)


def whole_kernel(
    nx, ny, groups,
    count, send, features, cotangent, rule, w1_in, w2_in,
    output, grad_input, grad_one, grad_two,
    feat, cot, rule3, w1, w2, flat, low, masks, columns,
    wide1, wide2, field, hidden, upstream, grad, pre, gathered, found, acc, own, sums,
    outs, backs, rets, gsend, prec, red, xrecv, ysend, yrecv,
    load_s, halo_ss, halo_rs, pss, prs, xss, xrs, yss, yrs,
):
    a, b = lax.axis_index("gx"), lax.axis_index("gy")
    nblk, blk, channels = field.shape
    rows = nblk * blk
    kernel = w1.shape[0]
    mid = kernel // 2
    per = send.shape[0]
    slot = per * blk
    chunk = channels // nx
    depth = acc.shape[0]
    first_slots = (depth - rows) // slot
    zero_row = rows + 8 * slot
    core = lax.rem(a, 2)
    chip = a // 2
    chips = nx // 2
    hops = ysend.shape[1]

    def exists(e):
        dx, dy = DIRECTIONS[e]
        x, y = a + dx, b + dy
        return (x >= 0) & (x < nx) & (y >= 0) & (y < ny)

    def place(e):
        dx, dy = DIRECTIONS[e]
        return (a + dx, b + dy)

    loads = [
        pltpu.make_async_copy(src, dst, load_s.at[n])
        for n, (src, dst) in enumerate((
            (features, feat), (rule, rule3), (cotangent, cot), (w2_in, w2), (w1_in, w1),
        ))
    ]
    for copy in loads:
        copy.start()

    barrier = pltpu.get_barrier_semaphore()
    for off in range(1, nx):
        pl.semaphore_signal(barrier, inc=1, device_id=(lax.rem(a + off, nx), b), device_id_type=MESH)
    for off in range(1, ny):
        pl.semaphore_signal(barrier, inc=1, device_id=(a, lax.rem(b + off, ny)), device_id_type=MESH)
    corners = (0, 2, 5, 7)
    for e in corners:
        dx, dy = DIRECTIONS[e]
        corner = (lax.rem(a + dx + nx, nx), lax.rem(b + dy + ny, ny))
        pl.semaphore_signal(barrier, inc=1, device_id=corner, device_id_type=MESH)

    def wide_view(wide, j):
        if j < first_slots:
            return wide.at[pl.ds(rows + j * slot, slot), pl.ds(0, channels)]
        return wide.at[pl.ds((j - first_slots) * slot, slot), pl.ds(channels, channels)]

    for j in range(8):
        @pl.when(jnp.logical_not(exists(j)))
        def _():
            blank = jnp.zeros((slot, channels), BF16)
            wide_view(wide1, j)[...] = blank
            wide_view(wide2, j)[...] = blank
            rets[0, j] = blank
            rets[1, j] = blank

    loads[0].wait()
    ids = lax.broadcasted_iota(jnp.int32, (rows, 1), 0)
    live = (ids < count[0, 0] * blk).astype(F32)
    masked32 = feat[...].astype(F32) * live
    masked = masked32.astype(BF16)
    field[...] = masked.reshape(nblk, blk, channels)
    wide1[:rows, :channels] = masked

    def ext_copy(x, e, wide):
        return pltpu.make_async_remote_copy(
            src_ref=outs.at[x, e], dst_ref=wide_view(wide, 7 - e),
            send_sem=halo_ss.at[x, e], recv_sem=halo_rs.at[x, 7 - e],
            device_id=place(e), device_id_type=MESH,
        )

    def back_copy(x, j):
        return pltpu.make_async_remote_copy(
            src_ref=backs.at[x, j], dst_ref=rets.at[x, j],
            send_sem=halo_ss.at[2 + x, j], recv_sem=halo_rs.at[2 + x, j],
            device_id=place(j), device_id_type=MESH,
        )

    def pack_ext(x, source):
        @pl.loop(0, 8)
        def _(e):
            for s in range(per):
                outs[x, e, s * blk : (s + 1) * blk, :] = source[send[s, e]]

    def start_ext(x, wide):
        for e in range(8):
            @pl.when(exists(e))
            def _():
                ext_copy(x, e, wide).start()

    def wait_ext(x, wide):
        for e in range(8):
            @pl.when(exists(7 - e))
            def _():
                ext_copy(x, e, wide).wait_recv()

    def send_back(x):
        for j in range(8):
            backs[x, j] = wide_view(acc, j)[...].astype(BF16)

            @pl.when(exists(j))
            def _():
                back_copy(x, j).start()

    def wait_back(x):
        for j in range(8):
            @pl.when(exists(7 - j))
            def _():
                back_copy(x, j).wait_recv()

    def returned_total(x):
        part = 32

        @pl.loop(0, blk // part)
        def _(h):
            here = pl.multiple_of(h * part, part)
            totals = [own[pl.ds(n * blk + here, part), :] for n in range(nblk)]
            for e in range(8):
                for s in range(per):
                    value = rets[x, e, pl.ds(s * blk + here, part), :].astype(F32)
                    target = send[s, 7 - e]
                    for n in range(nblk):
                        totals[n] += jnp.where(target == n, 1.0, 0.0) * value
            for n in range(nblk):
                own[pl.ds(n * blk + here, part), :] = totals[n]

    pack_ext(0, field)
    pl.semaphore_wait(barrier, nx - 1 + ny - 1 + len(corners))
    start_ext(0, wide1)

    loads[1].wait()
    for k in range(kernel):
        flat[k : k + 1, :] = rule3[k]
    flat[kernel:, :] = jnp.full((flat.shape[0] - kernel, rows), zero_row, jnp.int32)
    book = flat[...]
    second = book >= depth
    low[...] = jnp.where(second, book - depth, book)
    chosen = jnp.where(second, 1.0, 0.0).astype(BF16)
    within = jnp.where(second, book - depth, book)
    digits = jnp.concatenate([within // 256, lax.rem(within, 256)], axis=0).astype(F32).astype(BF16)
    shown = (flat.shape[0], 2 * channels)
    lanes_of = lax.broadcasted_iota(jnp.int32, shown, 1)
    rows_of = lax.broadcasted_iota(jnp.int32, shown, 0)

    @pl.loop(0, mid)
    def _(s):
        offset = jnp.where(lanes_of < channels, s, s + mid + 1)
        picks = jnp.where(rows_of == offset, 1.0, 0.0).astype(BF16)
        masks[s] = lax.dot_general(
            chosen, picks, (((0,), (0,)), ((), ())), preferred_element_type=F32
        ).astype(BF16)
        weighted = jnp.concatenate([picks * 256.0, picks], axis=0)
        columns[s] = lax.dot_general(
            digits, weighted, (((0,), (0,)), ((), ())), preferred_element_type=F32
        ).astype(jnp.int32).astype(I16)

    loads[2].wait()
    upstream[...] = (cot[...].astype(F32) * live).astype(BF16)
    loads[3].wait()
    loads[4].wait()

    def pair(s):
        return (s, s + mid + 1)

    def stacked(w, s):
        return jnp.concatenate([w[k] for k in pair(s)], axis=0)

    def scatter(s, g, w):
        terms = lax.dot_general(
            g, stacked(w, s), (((1,), (1,)), ((), ())), preferred_element_type=F32
        ).astype(BF16)
        upper = terms * masks[s]
        lower = terms - upper
        values = jnp.concatenate(
            [
                jnp.concatenate(
                    [part[:, u * channels : (u + 1) * channels] for part in (lower, upper)], axis=1
                )
                for u in range(2)
            ],
            axis=0,
        )
        place_of = lax.broadcasted_iota(I16, (depth, rows), 0)
        hots = []
        for k in pair(s):
            wanted = jnp.broadcast_to(low[pl.ds(k, 1), :].astype(I16), (depth, rows))
            hots.append(jnp.where(place_of == wanted, jnp.ones((), BF16), jnp.zeros((), BF16)))
        acc[...] += jnp.dot(jnp.concatenate(hots, axis=1), values, preferred_element_type=F32)

    def scatter_first(g, w):
        acc[...] = jnp.zeros_like(acc)
        acc[:rows, :channels] = lax.dot_general(
            g, w[mid], (((1,), (1,)), ((), ())), preferred_element_type=F32
        )

    def gather_dots(s, wide):
        lanes = lax.broadcasted_iota(I16, (rows, channels), 1)
        hots = []
        for u in range(2):
            wanted = columns[s, :, u * channels : (u + 1) * channels]
            hots.append(jnp.concatenate(
                [
                    jnp.where(wanted == lanes + I16(t * channels), jnp.ones((), BF16), jnp.zeros((), BF16))
                    for t in range(depth // channels)
                ],
                axis=1,
            ))
        sums_of = jnp.dot(jnp.concatenate(hots, axis=0), wide[...], preferred_element_type=F32)
        for u in range(2):
            upper = masks[s, :, u * channels : (u + 1) * channels].astype(F32) > 0.5
            part = sums_of[u * rows : (u + 1) * rows]
            found[:, u * channels : (u + 1) * channels] = jnp.where(
                upper, part[:, channels:], part[:, :channels]
            ).astype(BF16)

    def clear():
        found[...] = jnp.zeros_like(found)

    def keep(s, picks):
        for u, k in enumerate(pair(s)):
            gathered[k] = picks[:, u * channels : (u + 1) * channels]
        return picks

    def settle_dots(s):
        return keep(s, found[...])

    def both(s):
        return jnp.concatenate([gathered[k] for k in pair(s)], axis=1)

    def keep_partial(g, at, picks, rows_out):
        part = lax.dot_general(
            picks, rows_out, (((0,), (0,)), ((), ())), preferred_element_type=F32
        ).astype(BF16)
        for u in range(2):
            for p in range(nx):
                first = u * channels + p * chunk
                gsend[g, p % 2, p // 2, 1 + 2 * at + u] = part[first : first + chunk, :]

    def keep_first(g, rows_in, rows_out):
        part = lax.dot_general(
            rows_in, rows_out, (((0,), (0,)), ((), ())), preferred_element_type=F32
        ).astype(BF16)
        for p in range(nx):
            gsend[g, p % 2, p // 2, 0] = part[p * chunk : (p + 1) * chunk, :]

    def span(t):
        g, first, last = groups[t]
        return g, pl.ds(first, last - first)

    def pair_copy(t):
        g, qs = span(t)
        return pltpu.make_async_remote_copy(
            src_ref=gsend.at[g, 1 - core, :, qs], dst_ref=prec.at[g, :, qs],
            send_sem=pss.at[t], recv_sem=prs.at[t],
            device_id=(a + 1 - 2 * core, b), device_id_type=MESH,
        )

    def chip_copy(t, off):
        g, qs = span(t)
        peer = lax.rem(chip + off, chips)
        return pltpu.make_async_remote_copy(
            src_ref=red.at[g, peer, qs], dst_ref=xrecv.at[g, off, qs],
            send_sem=xss.at[t, off], recv_sem=xrs.at[t, off],
            device_id=(2 * peer + core, b), device_id_type=MESH,
        )

    def gy_copy(t, n):
        g, qs = span(t)
        step = 1 << n
        return pltpu.make_async_remote_copy(
            src_ref=ysend.at[g, n, qs], dst_ref=yrecv.at[g, n, qs],
            send_sem=yss.at[t, n], recv_sem=yrs.at[t, n],
            device_id=(a, b + step * (1 - 2 * lax.rem(b // step, 2))), device_id_type=MESH,
        )

    def reduce_pair(t):
        g, qs = span(t)
        pair_copy(t).wait_recv()
        for n in range(chips):
            red[g, n, qs] = (gsend[g, core, n, qs].astype(F32) + prec[g, n, qs].astype(F32)).astype(BF16)
        for off in range(1, chips):
            chip_copy(t, off).start()

    def reduce_chips(t):
        g, qs = span(t)
        total = red[g, chip, qs].astype(F32)
        for off in range(1, chips):
            chip_copy(t, off).wait_recv()
            total += xrecv[g, off, qs].astype(F32)
        ysend[g, 0, qs] = total.astype(BF16)
        gy_copy(t, 0).start()

    def reduce_gy(t, n):
        g, first, last = groups[t]
        _, qs = span(t)
        gy_copy(t, n).wait_recv()
        total = ysend[g, n, qs].astype(F32) + yrecv[g, n, qs].astype(F32)
        if n + 1 < hops:
            ysend[g, n + 1, qs] = total.astype(BF16)
            gy_copy(t, n + 1).start()
            return
        total = total * (1.0 / (nx * ny))
        out = (grad_one, grad_two)[g]
        for q in range(first, last):
            k = mid if q == 0 else (q - 1) // 2 + ((q - 1) % 2) * (mid + 1)
            out[k] = total[q - first]

    scatter_first(upstream[...], w2)

    @pl.loop(0, EARLY)
    def _(s):
        scatter(s, upstream[...], w2)

    clear()
    wait_ext(0, wide1)
    pre[...] = jnp.dot(wide1[:rows, :channels], w1[mid], preferred_element_type=F32)

    def first_conv(s, picks):
        pre[...] += jnp.dot(picks, stacked(w1, s), preferred_element_type=F32)

    beside = mid - EARLY

    def before(s):
        return jnp.where(s == 0, mid - 1, s - 1)

    @pl.loop(0, beside)
    def _(s):
        first_conv(before(s), settle_dots(before(s)))
        scatter(s + EARLY, upstream[...], w2)
        gather_dots(s, wide1)

    send_back(0)
    own[...] = acc[:rows, :channels]

    @pl.loop(beside, mid)
    def _(s):
        first_conv(s - 1, settle_dots(s - 1))
        gather_dots(s, wide1)

    first_conv(mid - 1, settle_dots(mid - 1))
    v = pre[...] * live
    pre[...] = v
    hid = (v / (1.0 + jnp.exp(-v))).astype(BF16)
    hidden[...] = hid.reshape(nblk, blk, channels)
    wide2[:rows, :channels] = hid
    pack_ext(1, hidden)
    start_ext(1, wide2)

    wait_back(0)
    returned_total(0)
    v = pre[...]
    s = 1.0 / (1.0 + jnp.exp(-v))
    grad[...] = (own[...] * s * (1.0 + v * (1.0 - s)) * live).astype(BF16)

    keep_first(0, wide1[:rows, :channels], grad[...])
    keep_partial(0, mid - 1, both(mid - 1), grad[...])
    scatter_first(grad[...], w1)

    @pl.loop(0, EARLY)
    def _(s):
        scatter(s, grad[...], w1)
        for n in range(2):
            keep_partial(0, 2 * s + n, both(2 * s + n), grad[...])

    pair_copy(0).start()
    clear()
    wait_ext(1, wide2)
    sums[...] = jnp.dot(wide2[:rows, :channels], w2[mid], preferred_element_type=F32)
    keep_first(1, wide2[:rows, :channels], upstream[...])

    def second_conv(s):
        picks = settle_dots(s)
        sums[...] += jnp.dot(picks, stacked(w2, s), preferred_element_type=F32)
        keep_partial(1, s, picks, upstream[...])

    @pl.loop(0, mid)
    def _(s):
        @pl.when(s == 2)
        def _():
            reduce_pair(0)

        @pl.when(s == beside + 1)
        def _():
            pair_copy(1).start()

        @pl.when(s == beside + 3)
        def _():
            reduce_pair(1)
            reduce_chips(0)

        second_conv(before(s))
        gather_dots(s, wide2)

    second_conv(mid - 1)
    pair_copy(2).start()
    reduce_gy(0, 0)
    output[...] = (sums[...] * live).astype(BF16)

    @pl.loop(EARLY, mid)
    def _(s):
        @pl.when(s == EARLY + 2)
        def _():
            reduce_pair(2)
            reduce_chips(1)

        @pl.when(s == EARLY + 5)
        def _():
            reduce_gy(1, 0)
            reduce_chips(2)

        scatter(s, grad[...], w1)

    send_back(1)
    own[...] = acc[:rows, :channels]
    reduce_gy(2, 0)
    for t in range(2):
        for n in range(1, hops):
            reduce_gy(t, n)
    wait_back(1)
    returned_total(1)
    grad_input[...] = (own[...] * live).astype(BF16)
    for n in range(1, hops):
        reduce_gy(2, n)

    for e in range(8):
        @pl.when(exists(e))
        def _():
            ext_copy(0, e, wide1).wait_send()
            ext_copy(1, e, wide2).wait_send()
            back_copy(0, e).wait_send()
            back_copy(1, e).wait_send()
    for t in range(len(groups)):
        pair_copy(t).wait_send()
        for off in range(1, chips):
            chip_copy(t, off).wait_send()
        for n in range(hops):
            gy_copy(t, n).wait_send()


def move_kernel(*refs):
    for n in range(4):
        refs[4 + n][...] = refs[n][...]


def on_device(features, cotangent, weight_one, weight_two, block_count, send_list, rulebook):
    field, cot = features[0, 0], cotangent[0, 0]
    rows, channels = field.shape
    kernel = rulebook.shape[2]
    mid = kernel // 2
    send = send_list[0, 0].T
    rule = rulebook.reshape(kernel, 1, rows)
    slot = send.shape[0] * BLK
    nx, ny = lax.axis_size("gx"), lax.axis_size("gy")
    chunk = channels // nx
    depth = (rows + 8 * slot) // 2
    split = 1 + 2 * (mid - EARLY)
    groups = ((0, 0, kernel), (1, 0, split), (1, split, kernel))
    hops = (ny - 1).bit_length()
    shape = jax.ShapeDtypeStruct
    grads = shape((kernel, chunk, channels), F32)
    plain_f = pltpu.VMEM((rows, channels), F32)
    plain_b = pltpu.VMEM((rows, channels), BF16)
    blocks = pltpu.VMEM((rows // BLK, BLK, channels), BF16)
    halos = pltpu.VMEM((2, 8, slot, channels), BF16)
    wide = pltpu.VMEM((depth, 2 * channels), BF16)
    weights = pltpu.VMEM((kernel, channels, channels), BF16)
    high = -(-kernel // 8) * 8
    parts = len(groups)
    tile = (chunk, channels)
    sem = pltpu.SemaphoreType.DMA
    output, grad_input, one, two = pl.pallas_call(
        functools.partial(whole_kernel, nx, ny, groups),
        out_shape=(shape((rows, channels), BF16),) * 2 + (grads, grads),
        in_specs=[SM, SM] + [ANY] * 5,
        out_specs=(VM,) * 4,
        scratch_shapes=[
            plain_b, plain_b, pltpu.VMEM((kernel, 1, rows), jnp.int32), weights, weights,
            pltpu.VMEM((high, rows), jnp.int32), pltpu.VMEM((high, rows), jnp.int32),
            pltpu.VMEM((mid, rows, 2 * channels), BF16),
            pltpu.VMEM((mid, rows, 2 * channels), I16),
            wide, wide, blocks, blocks,
            plain_b, plain_b, plain_f, pltpu.VMEM((kernel, rows, channels), BF16),
            pltpu.VMEM((rows, 2 * channels), BF16),
            pltpu.VMEM((depth, 2 * channels), F32),
            plain_f, plain_f, halos, halos, halos,
            pltpu.VMEM((2, 2, nx // 2, kernel) + tile, BF16),
            pltpu.VMEM((2, nx // 2, kernel) + tile, BF16),
            pltpu.VMEM((2, nx // 2, kernel) + tile, BF16),
            pltpu.VMEM((2, nx // 2, kernel) + tile, BF16),
            pltpu.VMEM((2, hops, kernel) + tile, BF16),
            pltpu.VMEM((2, hops, kernel) + tile, BF16),
            sem((6,)), sem((4, 8)), sem((4, 8)), sem((parts,)), sem((parts,)),
            sem((parts, nx // 2)), sem((parts, nx // 2)), sem((parts, hops)), sem((parts, hops)),
        ],
        compiler_params=pltpu.CompilerParams(
            vmem_limit_bytes=56 << 20, collective_id=0, has_side_effects=True
        ),
    )(block_count, send, field, cot, rule, weight_one, weight_two)
    results = (output, grad_input, one, two)
    output, grad_input, one, two = pl.pallas_call(
        move_kernel,
        out_shape=tuple(shape(x.shape, x.dtype) for x in results),
        in_specs=[VM] * 4,
        out_specs=(VM,) * 4,
    )(*results)
    return output[None, None], grad_input[None, None], one, two


def solution(mesh):
    placed = (
        P("gx", "gy", None, None),
        P("gx", "gy", None, None),
        P(),
        P(),
        P("gx", "gy"),
        P("gx", "gy", None, None),
        P("gx", "gy", None, None),
    )
    return jax.shard_map(
        on_device,
        mesh=mesh,
        in_specs=placed,
        out_specs=(
            P("gx", "gy", None, None),
            P("gx", "gy", None, None),
            P(None, "gx", None),
            P(None, "gx", None),
        ),
        check_vma=False,
    )
```

```python
import functools

import jax
import jax.numpy as jnp
from jax import lax
from jax.experimental import pallas as pl
from jax.experimental.pallas import tpu as pltpu
from jax.sharding import PartitionSpec as P

BLK = 64
EARLY = 6
F32 = jnp.float32
BF16 = jnp.bfloat16
I16 = jnp.int16
MESH = pl.DeviceIdType.MESH
DIRECTIONS = ((-1, -1), (-1, 0), (-1, 1), (0, -1), (0, 1), (1, -1), (1, 0), (1, 1))

VM = pl.BlockSpec(memory_space=pltpu.VMEM)
SM = pl.BlockSpec(memory_space=pltpu.SMEM)
ANY = pl.BlockSpec(memory_space=pl.ANY)


def whole_kernel(
    nx, ny, groups,
    count, send, features, cotangent, rule, w1_in, w2_in,
    output, grad_input, grad_one, grad_two,
    feat, cot, rule3, w1, w2, flat, low, masks, columns,
    wide1, wide2, field, hidden, upstream, grad, pre, gathered, found, acc, own, sums,
    outs, backs, rets, gsend, prec, red, xrecv, ysend, yrecv,
    load_s, halo_ss, halo_rs, pss, prs, xss, xrs, yss, yrs,
):
    a, b = lax.axis_index("gx"), lax.axis_index("gy")
    nblk, blk, channels = field.shape
    rows = nblk * blk
    kernel = w1.shape[0]
    mid = kernel // 2
    per = send.shape[0]
    slot = per * blk
    chunk = channels // nx
    depth = acc.shape[0]
    first_slots = (depth - rows) // slot
    zero_row = rows + 8 * slot
    core = lax.rem(a, 2)
    chip = a // 2
    chips = nx // 2
    hops = ysend.shape[1]

    def exists(e):
        dx, dy = DIRECTIONS[e]
        x, y = a + dx, b + dy
        return (x >= 0) & (x < nx) & (y >= 0) & (y < ny)

    def place(e):
        dx, dy = DIRECTIONS[e]
        return (a + dx, b + dy)

    loads = [
        pltpu.make_async_copy(src, dst, load_s.at[n])
        for n, (src, dst) in enumerate((
            (features, feat), (rule, rule3), (cotangent, cot), (w2_in, w2), (w1_in, w1),
        ))
    ]
    for copy in loads:
        copy.start()

    barrier = pltpu.get_barrier_semaphore()
    for off in range(1, nx):
        pl.semaphore_signal(barrier, inc=1, device_id=(lax.rem(a + off, nx), b), device_id_type=MESH)
    for off in range(1, ny):
        pl.semaphore_signal(barrier, inc=1, device_id=(a, lax.rem(b + off, ny)), device_id_type=MESH)
    corners = (0, 2, 5, 7)
    for e in corners:
        dx, dy = DIRECTIONS[e]
        corner = (lax.rem(a + dx + nx, nx), lax.rem(b + dy + ny, ny))
        pl.semaphore_signal(barrier, inc=1, device_id=corner, device_id_type=MESH)

    def wide_view(wide, j):
        if j < first_slots:
            return wide.at[pl.ds(rows + j * slot, slot), pl.ds(0, channels)]
        return wide.at[pl.ds((j - first_slots) * slot, slot), pl.ds(channels, channels)]

    for j in range(8):
        @pl.when(jnp.logical_not(exists(j)))
        def _():
            blank = jnp.zeros((slot, channels), BF16)
            wide_view(wide1, j)[...] = blank
            wide_view(wide2, j)[...] = blank
            rets[0, j] = blank
            rets[1, j] = blank

    loads[0].wait()
    ids = lax.broadcasted_iota(jnp.int32, (rows, 1), 0)
    live = (ids < count[0, 0] * blk).astype(F32)
    masked32 = feat[...].astype(F32) * live
    masked = masked32.astype(BF16)
    field[...] = masked.reshape(nblk, blk, channels)
    wide1[:rows, :channels] = masked

    def ext_copy(x, e, wide):
        return pltpu.make_async_remote_copy(
            src_ref=outs.at[x, e], dst_ref=wide_view(wide, 7 - e),
            send_sem=halo_ss.at[x, e], recv_sem=halo_rs.at[x, 7 - e],
            device_id=place(e), device_id_type=MESH,
        )

    def back_copy(x, j):
        return pltpu.make_async_remote_copy(
            src_ref=backs.at[x, j], dst_ref=rets.at[x, j],
            send_sem=halo_ss.at[2 + x, j], recv_sem=halo_rs.at[2 + x, j],
            device_id=place(j), device_id_type=MESH,
        )

    def pack_ext(x, source):
        @pl.loop(0, 8)
        def _(e):
            for s in range(per):
                outs[x, e, s * blk : (s + 1) * blk, :] = source[send[s, e]]

    def start_ext(x, wide):
        for e in range(8):
            @pl.when(exists(e))
            def _():
                ext_copy(x, e, wide).start()

    def wait_ext(x, wide):
        for e in range(8):
            @pl.when(exists(7 - e))
            def _():
                ext_copy(x, e, wide).wait_recv()

    def send_back(x):
        for j in range(8):
            backs[x, j] = wide_view(acc, j)[...].astype(BF16)

            @pl.when(exists(j))
            def _():
                back_copy(x, j).start()

    def wait_back(x):
        for j in range(8):
            @pl.when(exists(7 - j))
            def _():
                back_copy(x, j).wait_recv()

    def returned_total(x):
        part = 32

        @pl.loop(0, blk // part)
        def _(h):
            here = pl.multiple_of(h * part, part)
            totals = [own[pl.ds(n * blk + here, part), :] for n in range(nblk)]
            for e in range(8):
                for s in range(per):
                    value = rets[x, e, pl.ds(s * blk + here, part), :].astype(F32)
                    target = send[s, 7 - e]
                    for n in range(nblk):
                        totals[n] += jnp.where(target == n, 1.0, 0.0) * value
            for n in range(nblk):
                own[pl.ds(n * blk + here, part), :] = totals[n]

    pack_ext(0, field)
    pl.semaphore_wait(barrier, nx - 1 + ny - 1 + len(corners))
    start_ext(0, wide1)

    loads[1].wait()
    for k in range(kernel):
        flat[k : k + 1, :] = rule3[k]
    flat[kernel:, :] = jnp.full((flat.shape[0] - kernel, rows), zero_row, jnp.int32)
    book = flat[...]
    second = book >= depth
    low[...] = jnp.where(second, book - depth, book)
    chosen = jnp.where(second, 1.0, 0.0).astype(BF16)
    within = jnp.where(second, book - depth, book)
    digits = jnp.concatenate([within // 256, lax.rem(within, 256)], axis=0).astype(F32).astype(BF16)
    shown = (flat.shape[0], 2 * channels)
    lanes_of = lax.broadcasted_iota(jnp.int32, shown, 1)
    rows_of = lax.broadcasted_iota(jnp.int32, shown, 0)

    @pl.loop(0, mid)
    def _(s):
        offset = jnp.where(lanes_of < channels, s, s + mid + 1)
        picks = jnp.where(rows_of == offset, 1.0, 0.0).astype(BF16)
        masks[s] = lax.dot_general(
            chosen, picks, (((0,), (0,)), ((), ())), preferred_element_type=F32
        ).astype(BF16)
        weighted = jnp.concatenate([picks * 256.0, picks], axis=0)
        columns[s] = lax.dot_general(
            digits, weighted, (((0,), (0,)), ((), ())), preferred_element_type=F32
        ).astype(jnp.int32).astype(I16)

    loads[2].wait()
    upstream[...] = (cot[...].astype(F32) * live).astype(BF16)
    loads[3].wait()

    def pair(s):
        return (s, s + mid + 1)

    def stacked(w, s):
        return jnp.concatenate([w[k] for k in pair(s)], axis=0)

    def scatter(s, g, w):
        terms = lax.dot_general(
            g, stacked(w, s), (((1,), (1,)), ((), ())), preferred_element_type=F32
        ).astype(BF16)
        upper = terms * masks[s]
        lower = terms - upper
        values = jnp.concatenate(
            [
                jnp.concatenate(
                    [part[:, u * channels : (u + 1) * channels] for part in (lower, upper)], axis=1
                )
                for u in range(2)
            ],
            axis=0,
        )
        place_of = lax.broadcasted_iota(I16, (depth, rows), 0)
        hots = []
        for k in pair(s):
            wanted = jnp.broadcast_to(low[pl.ds(k, 1), :].astype(I16), (depth, rows))
            hots.append(jnp.where(place_of == wanted, jnp.ones((), BF16), jnp.zeros((), BF16)))
        acc[...] += jnp.dot(jnp.concatenate(hots, axis=1), values, preferred_element_type=F32)

    def scatter_first(g, w):
        acc[...] = jnp.zeros_like(acc)
        acc[:rows, :channels] = lax.dot_general(
            g, w[mid], (((1,), (1,)), ((), ())), preferred_element_type=F32
        )

    def gather_dots(s, wide):
        lanes = lax.broadcasted_iota(I16, (rows, channels), 1)
        hots = []
        for u in range(2):
            wanted = columns[s, :, u * channels : (u + 1) * channels]
            hots.append(jnp.concatenate(
                [
                    jnp.where(wanted == lanes + I16(t * channels), jnp.ones((), BF16), jnp.zeros((), BF16))
                    for t in range(depth // channels)
                ],
                axis=1,
            ))
        sums_of = jnp.dot(jnp.concatenate(hots, axis=0), wide[...], preferred_element_type=F32)
        for u in range(2):
            upper = masks[s, :, u * channels : (u + 1) * channels].astype(F32) > 0.5
            part = sums_of[u * rows : (u + 1) * rows]
            found[:, u * channels : (u + 1) * channels] = jnp.where(
                upper, part[:, channels:], part[:, :channels]
            ).astype(BF16)

    def clear():
        found[...] = jnp.zeros_like(found)

    def keep(s, picks):
        for u, k in enumerate(pair(s)):
            gathered[k] = picks[:, u * channels : (u + 1) * channels]
        return picks

    def settle_dots(s):
        return keep(s, found[...])

    def both(s):
        return jnp.concatenate([gathered[k] for k in pair(s)], axis=1)

    def keep_partial(g, at, picks, rows_out):
        part = lax.dot_general(
            picks, rows_out, (((0,), (0,)), ((), ())), preferred_element_type=F32
        ).astype(BF16)
        for u in range(2):
            for p in range(nx):
                first = u * channels + p * chunk
                gsend[g, p % 2, p // 2, 1 + 2 * at + u] = part[first : first + chunk, :]

    def keep_first(g, rows_in, rows_out):
        part = lax.dot_general(
            rows_in, rows_out, (((0,), (0,)), ((), ())), preferred_element_type=F32
        ).astype(BF16)
        for p in range(nx):
            gsend[g, p % 2, p // 2, 0] = part[p * chunk : (p + 1) * chunk, :]

    def span(t):
        g, first, last = groups[t]
        return g, pl.ds(first, last - first)

    def pair_copy(t):
        g, qs = span(t)
        return pltpu.make_async_remote_copy(
            src_ref=gsend.at[g, 1 - core, :, qs], dst_ref=prec.at[g, :, qs],
            send_sem=pss.at[t], recv_sem=prs.at[t],
            device_id=(a + 1 - 2 * core, b), device_id_type=MESH,
        )

    def chip_copy(t, off):
        g, qs = span(t)
        peer = lax.rem(chip + off, chips)
        return pltpu.make_async_remote_copy(
            src_ref=red.at[g, peer, qs], dst_ref=xrecv.at[g, off, qs],
            send_sem=xss.at[t, off], recv_sem=xrs.at[t, off],
            device_id=(2 * peer + core, b), device_id_type=MESH,
        )

    def gy_copy(t, n):
        g, qs = span(t)
        step = 1 << n
        return pltpu.make_async_remote_copy(
            src_ref=ysend.at[g, n, qs], dst_ref=yrecv.at[g, n, qs],
            send_sem=yss.at[t, n], recv_sem=yrs.at[t, n],
            device_id=(a, b + step * (1 - 2 * lax.rem(b // step, 2))), device_id_type=MESH,
        )

    def reduce_pair(t):
        g, qs = span(t)
        pair_copy(t).wait_recv()
        for n in range(chips):
            red[g, n, qs] = (gsend[g, core, n, qs].astype(F32) + prec[g, n, qs].astype(F32)).astype(BF16)
        for off in range(1, chips):
            chip_copy(t, off).start()

    def reduce_chips(t):
        g, qs = span(t)
        total = red[g, chip, qs].astype(F32)
        for off in range(1, chips):
            chip_copy(t, off).wait_recv()
            total += xrecv[g, off, qs].astype(F32)
        ysend[g, 0, qs] = total.astype(BF16)
        gy_copy(t, 0).start()

    def reduce_gy(t, n):
        g, first, last = groups[t]
        _, qs = span(t)
        gy_copy(t, n).wait_recv()
        total = ysend[g, n, qs].astype(F32) + yrecv[g, n, qs].astype(F32)
        if n + 1 < hops:
            ysend[g, n + 1, qs] = total.astype(BF16)
            gy_copy(t, n + 1).start()
            return
        total = total * (1.0 / (nx * ny))
        out = (grad_one, grad_two)[g]
        for q in range(first, last):
            k = mid if q == 0 else (q - 1) // 2 + ((q - 1) % 2) * (mid + 1)
            out[k] = total[q - first]

    scatter_first(upstream[...], w2)

    @pl.loop(0, EARLY)
    def _(s):
        scatter(s, upstream[...], w2)

    loads[4].wait()
    clear()
    wait_ext(0, wide1)
    pre[...] = jnp.dot(wide1[:rows, :channels], w1[mid], preferred_element_type=F32)

    def first_conv(s, picks):
        pre[...] += jnp.dot(picks, stacked(w1, s), preferred_element_type=F32)

    beside = mid - EARLY

    def before(s):
        return jnp.where(s == 0, mid - 1, s - 1)

    @pl.loop(0, beside)
    def _(s):
        first_conv(before(s), settle_dots(before(s)))
        scatter(s + EARLY, upstream[...], w2)
        gather_dots(s, wide1)

    send_back(0)
    own[...] = acc[:rows, :channels]

    @pl.loop(beside, mid)
    def _(s):
        first_conv(s - 1, settle_dots(s - 1))
        gather_dots(s, wide1)

    first_conv(mid - 1, settle_dots(mid - 1))
    v = pre[...] * live
    pre[...] = v
    hid = (v / (1.0 + jnp.exp(-v))).astype(BF16)
    hidden[...] = hid.reshape(nblk, blk, channels)
    wide2[:rows, :channels] = hid
    pack_ext(1, hidden)
    start_ext(1, wide2)

    wait_back(0)
    returned_total(0)
    v = pre[...]
    s = 1.0 / (1.0 + jnp.exp(-v))
    grad[...] = (own[...] * s * (1.0 + v * (1.0 - s)) * live).astype(BF16)

    keep_first(0, wide1[:rows, :channels], grad[...])
    keep_partial(0, mid - 1, both(mid - 1), grad[...])
    scatter_first(grad[...], w1)

    @pl.loop(0, EARLY)
    def _(s):
        scatter(s, grad[...], w1)
        for n in range(2):
            keep_partial(0, 2 * s + n, both(2 * s + n), grad[...])

    pair_copy(0).start()
    clear()
    wait_ext(1, wide2)
    sums[...] = jnp.dot(wide2[:rows, :channels], w2[mid], preferred_element_type=F32)
    keep_first(1, wide2[:rows, :channels], upstream[...])

    def second_conv(s):
        picks = settle_dots(s)
        sums[...] += jnp.dot(picks, stacked(w2, s), preferred_element_type=F32)
        keep_partial(1, s, picks, upstream[...])

    @pl.loop(0, mid)
    def _(s):
        @pl.when(s == 2)
        def _():
            reduce_pair(0)

        @pl.when(s == beside + 1)
        def _():
            pair_copy(1).start()

        @pl.when(s == beside + 3)
        def _():
            reduce_pair(1)
            reduce_chips(0)

        second_conv(before(s))
        gather_dots(s, wide2)

    second_conv(mid - 1)
    pair_copy(2).start()
    reduce_gy(0, 0)
    output[...] = (sums[...] * live).astype(BF16)

    @pl.loop(EARLY, mid)
    def _(s):
        @pl.when(s == EARLY + 2)
        def _():
            reduce_pair(2)
            reduce_chips(1)

        @pl.when(s == EARLY + 5)
        def _():
            reduce_gy(1, 0)
            reduce_chips(2)

        scatter(s, grad[...], w1)

    send_back(1)
    own[...] = acc[:rows, :channels]
    reduce_gy(2, 0)
    for t in range(2):
        for n in range(1, hops):
            reduce_gy(t, n)
    wait_back(1)
    returned_total(1)
    grad_input[...] = (own[...] * live).astype(BF16)
    for n in range(1, hops):
        reduce_gy(2, n)

    for e in range(8):
        @pl.when(exists(e))
        def _():
            ext_copy(0, e, wide1).wait_send()
            ext_copy(1, e, wide2).wait_send()
            back_copy(0, e).wait_send()
            back_copy(1, e).wait_send()
    for t in range(len(groups)):
        pair_copy(t).wait_send()
        for off in range(1, chips):
            chip_copy(t, off).wait_send()
        for n in range(hops):
            gy_copy(t, n).wait_send()


def move_kernel(*refs):
    for n in range(4):
        refs[4 + n][...] = refs[n][...]


def on_device(features, cotangent, weight_one, weight_two, block_count, send_list, rulebook):
    field, cot = features[0, 0], cotangent[0, 0]
    rows, channels = field.shape
    kernel = rulebook.shape[2]
    mid = kernel // 2
    send = send_list[0, 0].T
    rule = rulebook.reshape(kernel, 1, rows)
    slot = send.shape[0] * BLK
    nx, ny = lax.axis_size("gx"), lax.axis_size("gy")
    chunk = channels // nx
    depth = (rows + 8 * slot) // 2
    split = 1 + 2 * (mid - EARLY)
    groups = ((0, 0, kernel), (1, 0, split), (1, split, kernel))
    hops = (ny - 1).bit_length()
    shape = jax.ShapeDtypeStruct
    grads = shape((kernel, chunk, channels), F32)
    plain_f = pltpu.VMEM((rows, channels), F32)
    plain_b = pltpu.VMEM((rows, channels), BF16)
    blocks = pltpu.VMEM((rows // BLK, BLK, channels), BF16)
    halos = pltpu.VMEM((2, 8, slot, channels), BF16)
    wide = pltpu.VMEM((depth, 2 * channels), BF16)
    weights = pltpu.VMEM((kernel, channels, channels), BF16)
    high = -(-kernel // 8) * 8
    parts = len(groups)
    tile = (chunk, channels)
    sem = pltpu.SemaphoreType.DMA
    output, grad_input, one, two = pl.pallas_call(
        functools.partial(whole_kernel, nx, ny, groups),
        out_shape=(shape((rows, channels), BF16),) * 2 + (grads, grads),
        in_specs=[SM, SM] + [ANY] * 5,
        out_specs=(VM,) * 4,
        scratch_shapes=[
            plain_b, plain_b, pltpu.VMEM((kernel, 1, rows), jnp.int32), weights, weights,
            pltpu.VMEM((high, rows), jnp.int32), pltpu.VMEM((high, rows), jnp.int32),
            pltpu.VMEM((mid, rows, 2 * channels), BF16),
            pltpu.VMEM((mid, rows, 2 * channels), I16),
            wide, wide, blocks, blocks,
            plain_b, plain_b, plain_f, pltpu.VMEM((kernel, rows, channels), BF16),
            pltpu.VMEM((rows, 2 * channels), BF16),
            pltpu.VMEM((depth, 2 * channels), F32),
            plain_f, plain_f, halos, halos, halos,
            pltpu.VMEM((2, 2, nx // 2, kernel) + tile, BF16),
            pltpu.VMEM((2, nx // 2, kernel) + tile, BF16),
            pltpu.VMEM((2, nx // 2, kernel) + tile, BF16),
            pltpu.VMEM((2, nx // 2, kernel) + tile, BF16),
            pltpu.VMEM((2, hops, kernel) + tile, BF16),
            pltpu.VMEM((2, hops, kernel) + tile, BF16),
            sem((6,)), sem((4, 8)), sem((4, 8)), sem((parts,)), sem((parts,)),
            sem((parts, nx // 2)), sem((parts, nx // 2)), sem((parts, hops)), sem((parts, hops)),
        ],
        compiler_params=pltpu.CompilerParams(
            vmem_limit_bytes=56 << 20, collective_id=0, has_side_effects=True
        ),
    )(block_count, send, field, cot, rule, weight_one, weight_two)
    results = (output, grad_input, one, two)
    output, grad_input, one, two = pl.pallas_call(
        move_kernel,
        out_shape=tuple(shape(x.shape, x.dtype) for x in results),
        in_specs=[VM] * 4,
        out_specs=(VM,) * 4,
    )(*results)
    return output[None, None], grad_input[None, None], one, two


def solution(mesh):
    placed = (
        P("gx", "gy", None, None),
        P("gx", "gy", None, None),
        P(),
        P(),
        P("gx", "gy"),
        P("gx", "gy", None, None),
        P("gx", "gy", None, None),
    )
    return jax.shard_map(
        on_device,
        mesh=mesh,
        in_specs=placed,
        out_specs=(
            P("gx", "gy", None, None),
            P("gx", "gy", None, None),
            P(None, "gx", None),
            P(None, "gx", None),
        ),
        check_vma=False,
    )
```
